32 devices in a mesh: gx: 8 (over z, core), gy: 4 (over y, x).
Axes of the slice: x: 2, y: 2, z: 4, core: 2. Of those that a mesh axis runs over, the one named last changes fastest.
Arguments:
- adjoint_forcing: float32 [16, 1536, 1536], P(None, 'gx', 'gy'), may hold values from -6 to 6
- courant_x: bfloat16 [16, 1536, 1536], P(None, 'gx', 'gy'), may hold values from -0.44921875 to 0.44921875
- courant_y: bfloat16 [16, 1536, 1536], P(None, 'gx', 'gy'), may hold values from -0.44921875 to 0.44921875
- vertical_mix: bfloat16 [16, 1536, 1536], P(None, 'gx', 'gy'), may hold values from 0.019897461 to 0.23925781
- tile_block: int32 [8192], replicated, may hold values from 0 to 36863, as said below
- injection_level: int32 [8192], P(('gx', 'gy')), may hold values from 0 to 15
- plume_profile: float32 [16, 16], replicated, may hold values from 0 to 1
- burn_weight: bfloat16 [8192, 6400], P(('gx', 'gy')), may hold values from 0.19921875 to 1
Outputs:
- adjoint_start: float32 [16, 1536, 1536], P(None, 'gx', 'gy')
- emission_gradient: bfloat16 [8192, 6400], P(('gx', 'gy'))
The draws below stay inside these ranges and needn't reach their ends.
Inputs may be any that keep to these rules, and one draw needn't show every extreme that they name: `tile_block`: the tiles of one device lie on the columns of exactly 16 different devices, exactly 16 of them on each of those.
All inputs are finite; a program needn't handle non-finite values.
Results may differ from the reference program's by a relative error of at most 0.001.
Values sent between devices are 32-bit elements; how exact they have to be, the bound alone decides.
No kernel may reach another device: no remote copies, remote signals or barrier semaphores. Data moves between devices by JAX's collectives and lax.ppermute only.
A program may use at most 192 MiB of HBM per device.

```python
import jax
import jax.numpy as jnp
from jax import lax

LEV = 16
CX = 192
CY = 384
TILES_DEV = 256
ITERS = 4
TB = 8
SUB = 100
NX = 1536
NY = 1536
SOURCES = 16
CAP = 16
TILES = 8192
FIRE = 6400
N_GX = 8
N_GY = 4


def draw_tile_block(key, part):
    processor_total = N_GX * N_GY
    key_hot, key_noise, key_order, key_local = jax.random.split(jax.random.fold_in(key, 17), 4)
    priority_order = jax.random.permutation(key_hot, processor_total)
    burning_extra_weight = jnp.where(priority_order < max(processor_total // 8, 1), 4096, 0).astype(jnp.int32)
    random_perturbation = jax.random.randint(key_noise, (processor_total, processor_total), 0, 1024)
    tile_priority_values = (random_perturbation + burning_extra_weight[None, :]) * processor_total + jnp.arange(processor_total, dtype=jnp.int32)[None, :]
    chosen = lax.top_k(tile_priority_values, SOURCES)[1].astype(jnp.int32)
    repeated = jnp.repeat(chosen, CAP, axis=1)
    shuffle = jax.random.randint(key_order, (processor_total, TILES_DEV), 0, 4096) * TILES_DEV + jnp.arange(TILES_DEV, dtype=jnp.int32)[None, :]
    slot_order = jnp.argsort(shuffle, axis=1)
    source = jnp.take_along_axis(repeated, slot_order, axis=1)
    per_x = CX // TB
    per_y = CY // TB
    local_block = jax.random.randint(key_local, (processor_total, TILES_DEV), 0, per_x * per_y)
    block_row = source // N_GY * per_x + local_block // per_y
    block_col = source % N_GY * per_y + local_block % per_y
    return (block_row * (NY // TB) + block_col).reshape(-1).astype(jnp.int32)


def place_ends(array, key, low, largest):
    longest = array.shape.index(max(array.shape))
    spots = []
    for shift in (0, 1):
        where = [jax.random.randint(jax.random.fold_in(key, axis), (), 0, length) for axis, length in enumerate(array.shape)]
        where[longest] = (where[longest] + shift) % array.shape[longest]
        spots.append(tuple(where))
    return array.at[spots[0]].set(low).at[spots[1]].set(largest)


def level_of(stream_key, shape, cuts, low, high):
    level, own = 1.0, jax.random.fold_in(stream_key, 6)
    for axis_at, parts in cuts:
        steps = jnp.exp(jax.random.uniform(jax.random.fold_in(own, axis_at), (parts,), jnp.float32, low / len(cuts), high / len(cuts)))
        level = level * jnp.repeat(steps, shape[axis_at] // parts).reshape([-1 if axis == axis_at else 1 for axis in range(len(shape))])
    return level


def gaussian(rng, dims, spread, reach, cuts=(), kind=jnp.bfloat16):
    level = level_of(rng, dims, cuts, -0.22, 0.18) if cuts else 1.0
    values = jax.random.normal(rng, dims, jnp.float32) * spread * level
    return jnp.minimum(jnp.maximum(values, -reach), reach).astype(kind)


def setup_inputs(seed: int = 0) -> dict:
    key_list = jax.random.split(jax.random.key(seed), 9)
    return {
        "adjoint_forcing": gaussian(key_list[0], (LEV, NX, NY), 1.0, 6.0, ((1, 8), (2, 4)), jnp.float32),
        "courant_x": jnp.clip(jax.random.uniform(key_list[1], (LEV, NX, NY), jnp.float32, -0.44921875, 0.44921875) * level_of(key_list[1], (LEV, NX, NY), ((1, 8), (2, 4)), -0.4, 0.0), -0.44921875, 0.44921875).astype(jnp.bfloat16),
        "courant_y": jnp.clip(jax.random.uniform(key_list[2], (LEV, NX, NY), jnp.float32, -0.44921875, 0.44921875) * level_of(key_list[2], (LEV, NX, NY), ((1, 8), (2, 4)), -0.4, 0.0), -0.44921875, 0.44921875).astype(jnp.bfloat16),
        "vertical_mix": jnp.clip(0.019897461 + 0.21936035 * jax.random.uniform(key_list[3], (LEV, NX, NY), jnp.float32) ** level_of(key_list[3], (LEV, NX, NY), ((1, 8), (2, 4)), -0.2, 0.2), 0.019897461, 0.23925781).astype(jnp.bfloat16),
        "tile_block": draw_tile_block(jax.random.fold_in(key_list[8], 71), 0),
        "injection_level": place_ends(jax.random.randint(key_list[5], (TILES,), 0, LEV), jax.random.fold_in(key_list[5], 1), 0, LEV - 1).astype(jnp.int32),
        "plume_profile": jnp.clip(jax.random.uniform(key_list[6], (LEV, LEV), jnp.float32, 0.0, 1.0), 0.0, 1.0),
        "burn_weight": jnp.clip(0.19921875 + 0.80078125 * jax.random.uniform(key_list[7], (TILES, FIRE), jnp.float32) ** level_of(key_list[7], (TILES, FIRE), ((0, 32),), -0.2, 0.2), 0.19921875, 1.0).astype(jnp.bfloat16),
    }


def diffuse(state_field, mixing):
    flux = mixing[:-1] * (state_field[1:] - state_field[:-1])
    zero_layer = jnp.zeros_like(state_field[:1])
    upper = jnp.concatenate([flux, zero_layer], 0)
    lower = jnp.concatenate([zero_layer, flux], 0)
    return state_field + upper - lower


def advect(padded, speed_x, speed_y):
    center = padded[:, 1:-1, 1:-1]
    keep = 1.0 - jnp.abs(speed_x) - jnp.abs(speed_y)
    total = keep * center
    total = total + jnp.maximum(speed_x, 0.0) * padded[:, 2:, 1:-1]
    total = total + jnp.maximum(-speed_x, 0.0) * padded[:, :-2, 1:-1]
    total = total + jnp.maximum(speed_y, 0.0) * padded[:, 1:-1, 2:]
    total = total + jnp.maximum(-speed_y, 0.0) * padded[:, 1:-1, :-2]
    return total


def reference(adjoint_forcing, courant_x, courant_y, vertical_mix, tile_block, injection_level, plume_profile, burn_weight):
    speed_x = courant_x.astype(jnp.float32)
    speed_y = courant_y.astype(jnp.float32)
    mixing = vertical_mix.astype(jnp.float32)
    state_field = adjoint_forcing
    for repeat_index in range(ITERS):
        blended_concentration = diffuse(state_field, mixing)
        padded = jnp.pad(blended_concentration, ((0, 0), (1, 1), (1, 1)))
        state_field = advect(padded, speed_x, speed_y)
    blocks_y = NY // TB
    row_starts = ((tile_block // blocks_y) * TB).astype(jnp.int32)
    col_starts = ((tile_block % blocks_y) * TB).astype(jnp.int32)

    def cut_block(start_row, start_col):
        piece = lax.dynamic_slice(state_field, (jnp.int32(0), start_row, start_col), (LEV, TB, TB))
        return piece.reshape(LEV, TB * TB)

    pieces = jax.vmap(cut_block)(row_starts, col_starts)
    onehot = (injection_level[:, None] == jnp.arange(LEV, dtype=jnp.int32)[None, :]).astype(jnp.float32)
    weights = jnp.dot(onehot, plume_profile, precision=lax.Precision.HIGHEST)
    column = jnp.einsum("kl,klc->kc", weights, pieces, precision=lax.Precision.HIGHEST)
    tiles_total = tile_block.shape[0]
    gradient = burn_weight.astype(jnp.float32).reshape(tiles_total, TB * TB, SUB) * column[:, :, None]
    return state_field, gradient.reshape(tiles_total, TB * TB * SUB).astype(jnp.bfloat16)
```

```python
import functools

import jax
import jax.numpy as jnp
from jax import lax
from jax.experimental import pallas as pl
from jax.experimental.pallas import tpu as pltpu
from jax.sharding import PartitionSpec as P

ITERS = 4
TB = 8
SUB = 100
LANES = 128
SUBL = 8
ROWS = 16
FRONT = 2 * ROWS
HALO = ITERS

F32 = jnp.float32
BF16 = jnp.bfloat16
I32 = jnp.int32
ANY = pl.BlockSpec(memory_space=pl.ANY)
VMEM = pl.BlockSpec(memory_space=pltpu.VMEM)
SMEM = pl.BlockSpec(memory_space=pltpu.SMEM)


def params(mib, **kw):
    return pltpu.CompilerParams(vmem_limit_bytes=mib << 20, **kw)


def cost(flops, nbytes):
    return pl.CostEstimate(flops=flops, bytes_accessed=nbytes, transcendentals=0)


def lane_id(shape):
    return lax.broadcasted_iota(I32, shape, 1)


def pack_x_kernel(vt, vb, cut, cub, cvt, cvb, kt, kb, up, dn):
    h, b = (HALO, ROWS)

    def level(l, _):
        up[0, l] = jnp.concatenate([vt[l, :h], cut[l].astype(F32)[:h]], 0)
        up[1, l] = jnp.concatenate([cvt[l].astype(F32)[:h], kt[l].astype(F32)[:h]], 0)
        dn[0, l] = jnp.concatenate([vb[l, SUBL - h :], cub[l].astype(F32)[b - h :]], 0)
        dn[1, l] = jnp.concatenate([cvb[l].astype(F32)[b - h :], kb[l].astype(F32)[b - h :]], 0)
        return 0

    lax.fori_loop(0, vt.shape[0], level, 0)


def pack_x(v, cu, cv, k):
    lev, nx, ny = v.shape

    def ends(x, rows):
        last = nx // rows - 1
        return (
            pl.BlockSpec((lev, rows, ny), lambda i: (0, 0, 0)),
            pl.BlockSpec((lev, rows, ny), lambda i: (0, last, 0)),
        )

    specs = [s for x, r in ((v, SUBL), (cu, ROWS), (cv, ROWS), (k, ROWS)) for s in ends(x, r)]
    out = jax.ShapeDtypeStruct((2, lev, 2 * HALO, ny), F32)
    whole = pl.BlockSpec((2, lev, 2 * HALO, ny), lambda i: (0, 0, 0, 0))
    return pl.pallas_call(
        pack_x_kernel,
        grid=(1,),
        out_shape=(out, out),
        in_specs=specs,
        out_specs=(whole, whole),
        compiler_params=params(12),
        cost_estimate=cost(0, 3 << 20),
        name="pack_x",
    )(v, v, cu, cu, cv, cv, k, k)


def edge_lanes(rows, lev, right):
    per = LANES // lev
    lane = lane_id((rows, LANES))
    take = lane // lev + (LANES - per if right else 0)
    return take, lane % lev


def pack_edge(slabs, take, level):
    acc = None
    for l, slab in enumerate(slabs):
        got = jnp.take_along_axis(slab, take, axis=1)
        acc = got if acc is None else jnp.where(level == l, got, acc)
    return acc


def store_edges(packed, own, send, at, right):
    v, cu, cv, k = packed
    for i, x in enumerate(packed):
        own[i, at, :] = x
    low = lane_id(v.shape) < LANES // 2
    half = LANES // 2
    for i, (a, b) in enumerate(((v, cu), (cv, k))):
        if right:
            send[i, at, :] = jnp.where(low, pltpu.roll(a, half, 1), b)
        else:
            send[i, at, :] = jnp.where(low, a, pltpu.roll(b, half, 1))


def pack_y_kernel(*refs):
    ins, outs = (refs[:8], refs[8:])
    lev, rows, _ = ins[0].shape
    for side in range(2):
        take, level = edge_lanes(ROWS, lev, side == 1)
        for r in range(rows // ROWS):
            at = slice(r * ROWS, (r + 1) * ROWS)
            packed = [
                pack_edge([ins[2 * a + side][l, at, :].astype(F32) for l in range(lev)], take, level)
                for a in range(4)
            ]
            store_edges(packed, outs[2 * side], outs[2 * side + 1], at, side == 1)


def pack_y(v, cu, cv, k):
    lev, nx, ny = v.shape
    nt = ny // LANES
    rows = 2 * ROWS
    left = pl.BlockSpec((lev, rows, LANES), lambda i: (0, i, 0))
    right = pl.BlockSpec((lev, rows, LANES), lambda i: (0, i, nt - 1))
    own = jax.ShapeDtypeStruct((4, nx + SUBL, LANES), F32)
    send = jax.ShapeDtypeStruct((2, nx + SUBL, LANES), F32)
    own_spec = pl.BlockSpec((4, rows, LANES), lambda i: (0, i, 0))
    send_spec = pl.BlockSpec((2, rows, LANES), lambda i: (0, i, 0))
    return pl.pallas_call(
        pack_y_kernel,
        grid=(nx // rows,),
        out_shape=(own, send, own, send),
        in_specs=[left, right] * 4,
        out_specs=(own_spec, send_spec, own_spec, send_spec),
        compiler_params=params(12),
        cost_estimate=cost(0, 10 << 20),
        name="pack_y",
    )(v, v, cu, cu, cv, cv, k, k)


def pack_corner_kernel(above, below, *refs):
    outs = refs[4:]
    lev, ny = (above.shape[1], above.shape[3])
    for side in range(2):
        take, level = edge_lanes(SUBL, lev, side == 1)
        lanes = slice(ny - LANES, ny) if side else slice(0, LANES)
        packed = []
        for q, o in ((0, 0), (0, HALO), (1, 0), (1, HALO)):
            slabs = [
                jnp.concatenate([below[q, l, o : o + HALO, lanes], above[q, l, o : o + HALO, lanes]], 0)
                for l in range(lev)
            ]
            packed.append(pack_edge(slabs, take, level))
        store_edges(packed, outs[2 * side], outs[2 * side + 1], slice(0, SUBL), side == 1)


def pack_corner(above, below, edges):
    last = edges[0].shape[1] // SUBL - 1
    specs = [
        pl.BlockSpec((x.shape[0], SUBL, LANES), lambda i: (0, last, 0)) for x in edges
    ]
    full = pl.BlockSpec(above.shape, lambda i: (0, 0, 0, 0))
    return pl.pallas_call(
        pack_corner_kernel,
        grid=(1,),
        out_shape=tuple(jax.ShapeDtypeStruct(x.shape, x.dtype) for x in edges),
        in_specs=[full, full] + [ANY] * 4,
        out_specs=tuple(specs),
        input_output_aliases={2 + i: i for i in range(4)},
        compiler_params=params(8),
        cost_estimate=cost(0, 1 << 20),
        name="pack_corner",
    )(above, below, *edges)


def stencil_kernel(v_hbm, cu_hbm, cv_hbm, k_hbm, ab, be, out_hbm, wa, wb, cub, cvb, kb, sem, osem, *, lev, nx, nt):
    srcs = ((v_hbm, wa), (k_hbm, kb), (cu_hbm, cub), (cv_hbm, cvb))
    copies = [
        [
            pltpu.make_async_copy(
                s.at[:, :, pl.ds(LANES * j, LANES)], d.at[:, j, pl.ds(FRONT, nx), :], sem.at[i, j]
            )
            for j in range(nt)
        ]
        for i, (s, d) in enumerate(srcs)
    ]
    for group in copies:
        for c in group:
            c.start()
    rest = jnp.zeros((ROWS - HALO, LANES), F32)

    def halo(l, _):
        for j in range(nt):
            lanes = slice(LANES * j, LANES * (j + 1))
            for buf, q, o in ((wa, 0, 0), (cub, 0, HALO), (cvb, 1, 0), (kb, 1, HALO)):
                top = ab[q, l, o : o + HALO, lanes]
                low = be[q, l, o : o + HALO, lanes]
                buf[l, j, FRONT - ROWS : FRONT, :] = jnp.concatenate([rest, top], 0).astype(buf.dtype)
                buf[l, j, FRONT + nx : FRONT + nx + ROWS, :] = jnp.concatenate([low, rest], 0).astype(buf.dtype)
        return 0

    lax.fori_loop(0, lev, halo, 0)
    lane = lane_id((ROWS, LANES))
    first, last = (lane == 0, lane == LANES - 1)

    def load(ref, l, j, r, off=0):
        if off:
            return ref[l, j, pl.ds(r * ROWS + off, ROWS), :]
        return ref[l, j, pl.ds(pl.multiple_of(r * ROWS, ROWS), ROWS), :]

    def advect(src, l, r):
        mid = [load(src, l, j, r) for j in range(nt)]
        nxt = [pltpu.roll(x, LANES - 1, 1) for x in mid]
        prv = [pltpu.roll(x, 1, 1) for x in mid]
        out = []
        for j in range(nt):
            yp = jnp.where(last, nxt[j + 1], nxt[j]) if j + 1 < nt else nxt[j]
            ym = jnp.where(first, prv[j - 1], prv[j]) if j > 0 else prv[j]
            cu = load(cub, l, j, r).astype(F32)
            cv = load(cvb, l, j, r).astype(F32)
            wx = jnp.where(cu > 0, load(src, l, j, r, 1), load(src, l, j, r, -1))
            wy = jnp.where(cv > 0, yp, ym)
            out.append(mid[j] + jnp.abs(cu) * (wx - mid[j]) + jnp.abs(cv) * (wy - mid[j]))
        return out

    def block(src, dst, do_b, do_d, r):
        def get(l):
            if l >= lev:
                return None
            return advect(src, l, r) if do_b else [load(src, l, j, r) for j in range(nt)]

        at = pl.ds(pl.multiple_of(r * ROWS, ROWS), ROWS)
        cur, below = (get(0), None)
        for l in range(lev):
            nxt = get(l + 1)
            flux = []
            for j in range(nt):
                w = cur[j]
                if do_d:
                    if nxt is not None:
                        f = load(kb, l, j, r).astype(F32) * (nxt[j] - cur[j])
                        flux.append(f)
                        w = w + (f - below[j]) if below else w + f
                    else:
                        w = w - below[j]
                dst[l, j, at, :] = w
            cur, below = (nxt, flux)

    def sweep(src, dst, do_b, do_d, lo, hi):
        def body(r, _):
            block(src, dst, do_b, do_d, r)
            return 0

        lax.fori_loop(lo, hi, body, 0)

    begin, end = (FRONT // ROWS, (FRONT + nx) // ROWS)
    for group in copies[:2]:
        for c in group:
            c.wait()
    sweep(wa, wb, False, True, begin - 1, end + 1)
    for group in copies[2:]:
        for c in group:
            c.wait()
    src, dst = (wb, wa)
    for _ in range(1, ITERS):
        sweep(src, dst, True, True, begin - 1, end + 1)
        src, dst = (dst, src)
    sweep(src, dst, True, False, begin, end)
    done = pltpu.make_async_copy(dst.at[:, :, pl.ds(FRONT, nx), :], out_hbm, osem)
    done.start()
    done.wait()


def stencil(v, cu, cv, k, above, below):
    lev, nx, ny = v.shape
    nt = ny // LANES
    shape = (lev, nt, nx + 2 * FRONT, LANES)
    return pl.pallas_call(
        functools.partial(stencil_kernel, lev=lev, nx=nx, nt=nt),
        out_shape=jax.ShapeDtypeStruct((lev, nt, nx, LANES), F32),
        in_specs=[ANY] * 4 + [VMEM] * 2,
        out_specs=ANY,
        scratch_shapes=[
            pltpu.VMEM(shape, F32),
            pltpu.VMEM(shape, F32),
            pltpu.VMEM(shape, BF16),
            pltpu.VMEM(shape, BF16),
            pltpu.VMEM(shape, BF16),
            pltpu.SemaphoreType.DMA((4, nt)),
            pltpu.SemaphoreType.DMA,
        ],
        compiler_params=params(40),
        cost_estimate=cost(90 * lev * nx * ny, 60 << 20),
        name="stencil",
    )(v, cu, cv, k, above, below)


def index_kernel(me_ref, blocks, row, shift, pos, src_col, slot_col, *, per_x, per_y, gy, cap, nx):
    procs, tiles = blocks.shape
    me = me_ref[0]
    per_tile = LANES // TB

    def owner(b):
        br, bc = (b // (per_y * gy), b % (per_y * gy))
        return br // per_x * gy + bc // per_y, br % per_x, bc % per_y

    src, lr, lc = owner(blocks[...])
    mine = src == me
    t = lane_id((procs, tiles))
    upper = lax.broadcasted_iota(I32, (tiles, tiles), 0) <= lane_id((tiles, tiles))
    rank = jnp.dot(
        mine.astype(F32).astype(BF16), upper.astype(F32).astype(BF16), preferred_element_type=F32
    ).astype(I32)
    code = ((lc // per_tile * nx + lr * TB) * per_tile + lc % per_tile) * tiles + t + 1
    lane = lane_id((procs, LANES))
    found = jnp.zeros((procs, LANES), I32)
    for s in range(cap):
        hit = mine & (rank == s + 1)
        one = jnp.sum(jnp.where(hit, code, 0).astype(F32), axis=1, keepdims=True).astype(I32)
        found = jnp.where(lane == s, one, found)
    value = found - 1
    spot = value // tiles
    row[...] = jnp.where(found > 0, spot // per_tile, -1)
    shift[...] = (lane * TB - spot % per_tile * TB) & (LANES - 1)
    pos[...] = value % tiles
    own = owner(blocks[pl.ds(me, 1), :])[0]
    i = lax.broadcasted_iota(I32, (tiles, tiles), 0)
    j = lane_id((tiles, tiles))
    own_all = jnp.broadcast_to(own, (tiles, tiles)).astype(F32)
    col = jnp.sum(jnp.where(i == j, own_all, 0.0), axis=1, keepdims=True)
    same = (own_all == col) & (j < i)
    src_col[...] = col.astype(I32)
    slot_col[...] = jnp.sum(jnp.where(same, 1.0, 0.0), axis=1, keepdims=True).astype(I32)


def tile_indices(me, blocks, cap, per_x, per_y, gy, nx):
    procs, tiles = blocks.shape
    table = jax.ShapeDtypeStruct((procs, LANES), I32)
    column = jax.ShapeDtypeStruct((tiles, 1), I32)
    return pl.pallas_call(
        functools.partial(index_kernel, per_x=per_x, per_y=per_y, gy=gy, cap=cap, nx=nx),
        out_shape=(table, table, table, column, column),
        in_specs=[SMEM, VMEM],
        out_specs=(VMEM,) * 5,
        compiler_params=params(8),
        cost_estimate=cost(0, 1 << 20),
        name="tile_indices",
    )(me, blocks)


def finish_kernel(
    me_ref, row, shift, pos, inj, prof, mid_hbm, own_l, own_r, got_l, got_r, state, send,
    field, strip, other, coef, sem, osem, *, lev, nx, nt, cap, procs,
):
    fetch = [
        pltpu.make_async_copy(mid_hbm.at[:, j], field.at[:, pl.ds(j * nx, nx), :], sem.at[j])
        for j in range(nt)
    ]
    for c in fetch:
        c.start()
    rows = nx + 2 * HALO
    step = rows // 5 if rows % 40 == 0 else SUBL
    half = LANES // 2
    lane = lane_id((step, LANES))
    low = lane < half
    top_level = lane % lev == lev - 1
    head, tail = (lane < lev, lane >= LANES - lev)

    def turn(x):
        return pltpu.roll(x, half, 1)

    def gather(n, _):
        at = pl.ds(pl.multiple_of(n * step, SUBL), step)
        put = pl.ds(pl.multiple_of(n * step + SUBL, SUBL), step)
        for a in range(4):
            q = a // 2
            ol, orr = (own_l[a, at, :], own_r[a, at, :])
            gl, gr = (got_l[q, at, :], got_r[q, at, :])
            if a % 2:
                gl = turn(gl)
            else:
                gr = turn(gr)
            parts = (
                jnp.where(low, gl, turn(ol)),
                turn(jnp.where(low, orr, ol)),
                jnp.where(low, turn(orr), gr),
            )
            for i, x in enumerate(parts):
                if a == 0:
                    strip[i, put, :] = x
                elif a == 3:
                    coef[2, i, at, :] = jnp.where(top_level, 0.0, x)
                else:
                    coef[a - 1, i, at, :] = x
        return 0

    lax.fori_loop(0, rows // step, gather, 0)

    def diffuse(n, _):
        at = pl.ds(pl.multiple_of(n * step, SUBL), step)
        put = pl.ds(pl.multiple_of(n * step + SUBL, SUBL), step)
        for i in range(3):
            x = strip[i, put, :]
            f = coef[2, i, at, :] * (pltpu.roll(x, LANES - 1, 1) - x)
            other[i, put, :] = x + f - pltpu.roll(f, 1, 1)
        return 0

    def advect(n, _):
        at = pl.ds(pl.multiple_of(n * step, SUBL), step)
        put = pl.ds(pl.multiple_of(n * step + SUBL, SUBL), step)
        mid = [other[i, put, :] for i in range(3)]
        nxt = [pltpu.roll(x, LANES - lev, 1) for x in mid]
        prv = [pltpu.roll(x, lev, 1) for x in mid]
        yps = (jnp.where(tail, nxt[1], nxt[0]), jnp.where(tail, nxt[2], nxt[1]), nxt[2])
        yms = (prv[0], jnp.where(head, prv[0], prv[1]), jnp.where(head, prv[1], prv[2]))
        for i in range(3):
            cu, cv = (coef[0, i, at, :], coef[1, i, at, :])
            wx = jnp.where(
                cu > 0,
                other[i, pl.ds(n * step + SUBL + 1, step), :],
                other[i, pl.ds(n * step + SUBL - 1, step), :],
            )
            wy = jnp.where(cv > 0, yps[i], yms[i])
            strip[i, put, :] = mid[i] + jnp.abs(cu) * (wx - mid[i]) + jnp.abs(cv) * (wy - mid[i])
        return 0

    for _ in range(ITERS):
        lax.fori_loop(0, rows // step, diffuse, 0)
        for i in range(3):
            other[i, SUBL - 1 : SUBL, :] = other[i, SUBL + rows - 1 : SUBL + rows, :]
            other[i, SUBL + rows : SUBL + rows + 1, :] = other[i, SUBL : SUBL + 1, :]
        lax.fori_loop(0, rows // step, advect, 0)

    for c in fetch:
        c.wait()
    lane16 = lane_id((ROWS, LANES))
    width = HALO

    def patch(n, _):
        put = pl.ds(pl.multiple_of(n * ROWS + SUBL, SUBL), ROWS)
        left, right = (strip[0, put, :], strip[2, put, :])
        for l in range(lev):
            take_l = (lane16 * lev + (half + l)) & (LANES - 1)
            take_r = ((lane16 - (LANES - width)) * lev + l) & (LANES - 1)
            a = pl.ds(pl.multiple_of(n * ROWS, ROWS), ROWS)
            b = pl.ds(pl.multiple_of((nt - 1) * nx + n * ROWS, ROWS), ROWS)
            field[l, a, :] = jnp.where(lane16 < width, jnp.take_along_axis(left, take_l, axis=1), field[l, a, :])
            field[l, b, :] = jnp.where(
                lane16 >= LANES - width, jnp.take_along_axis(right, take_r, axis=1), field[l, b, :]
            )
        return 0

    lax.fori_loop(0, nx // ROWS, patch, 0)
    puts = [
        pltpu.make_async_copy(
            field.at[:, pl.ds(j * nx, nx), :], state.at[:, :, pl.ds(j * LANES, LANES)], osem.at[j]
        )
        for j in range(nt)
    ]
    for c in puts:
        c.start()
    me = me_ref[0]
    slot_of = lane_id((TB, LANES)) // TB

    def handler(h, _):
        @pl.when(row[h, 0] >= 0)
        def _():
            out = jnp.zeros((TB, LANES), F32)
            source = h ^ me
            for s in range(cap):
                at = pl.ds(pl.multiple_of(row[h, s], TB), TB)
                level = inj[source, pos[h, s]]
                acc = prof[level, 0] * field[0, at, :]
                for l in range(1, lev):
                    acc = acc + prof[level, l] * field[l, at, :]
                out = jnp.where(slot_of == s, pltpu.roll(acc, shift[h, s], 1), out)
            send[h] = out

        @pl.when(row[h, 0] < 0)
        def _():
            send[h] = jnp.zeros((TB, LANES), F32)

        return 0

    lax.fori_loop(0, procs, handler, 0)
    for c in puts:
        c.wait()


def finish(me, row, shift, pos, inj, prof, mid, own_l, own_r, got_l, got_r, cap):
    lev, nt, nx, _ = mid.shape
    procs = row.shape[0]
    rows = nx + 2 * HALO
    return pl.pallas_call(
        functools.partial(finish_kernel, lev=lev, nx=nx, nt=nt, cap=cap, procs=procs),
        out_shape=(
            jax.ShapeDtypeStruct((lev, nx, nt * LANES), F32),
            jax.ShapeDtypeStruct((procs, TB, LANES), F32),
        ),
        in_specs=[SMEM] * 6 + [ANY] + [VMEM] * 4,
        out_specs=(ANY, VMEM),
        scratch_shapes=[
            pltpu.VMEM((lev, nt * nx, LANES), F32),
            pltpu.VMEM((3, rows + 2 * SUBL, LANES), F32),
            pltpu.VMEM((3, rows + 2 * SUBL, LANES), F32),
            pltpu.VMEM((3, 3, rows, LANES), F32),
            pltpu.SemaphoreType.DMA((nt,)),
            pltpu.SemaphoreType.DMA((nt,)),
        ],
        compiler_params=params(20),
        cost_estimate=cost(30 << 20, 20 << 20),
        name="finish",
    )(me, row, shift, pos, inj, prof, mid, own_l, own_r, got_l, got_r)


def split3(x):
    hi = x.astype(BF16)
    rest = x - hi.astype(F32)
    mid = rest.astype(BF16)
    return hi, mid, (rest - mid.astype(F32)).astype(BF16)


def gradient_kernel(src, slot, got, burn, out, cols, *, cells):
    tiles, width = burn.shape
    procs = got.shape[0]
    step = pl.program_id(0)

    @pl.when(step == 0)
    def _():
        pick = (src[...] == lane_id((tiles, procs))).astype(F32).astype(BF16)
        pick3 = jnp.concatenate([pick] * 3, 1)
        lane = lane_id((tiles, LANES))
        keep = lane // TB == slot[...]
        col = jnp.zeros((tiles, LANES), F32)
        for a in range(TB):
            parts = jnp.concatenate(split3(got[:, a, :]), 0)
            t = jnp.where(keep, jnp.dot(pick3, parts, preferred_element_type=F32), 0.0)
            w = LANES // 2
            while w >= TB:
                t = t + pltpu.roll(t, w, 1)
                w //= 2
            col = jnp.where(lane // TB == a, t, col)
        hi, mid, lo = split3(col[:, :cells])
        cols[...] = jnp.concatenate([hi, mid, lo], 1)

    q = step * width + lane_id((cells, width))
    c = lax.broadcasted_iota(I32, (cells, width), 0) * SUB
    spread = ((q >= c) & (q < c + SUB)).astype(F32).astype(BF16)
    wide = jnp.dot(cols[...], jnp.concatenate([spread] * 3, 0), preferred_element_type=F32)
    out[...] = (burn[...].astype(F32) * wide).astype(BF16)


def gradient(src, slot, got, burn):
    tiles, fire = burn.shape
    cells = TB * TB
    width = max(w for w in range(LANES, 11 * LANES, LANES) if fire % w == 0)
    block = pl.BlockSpec((tiles, width), lambda i: (0, i))
    return pl.pallas_call(
        functools.partial(gradient_kernel, cells=cells),
        grid=(fire // width,),
        out_shape=jax.ShapeDtypeStruct((tiles, fire), BF16),
        in_specs=[
            pl.BlockSpec((tiles, 1), lambda i: (0, 0)),
            pl.BlockSpec((tiles, 1), lambda i: (0, 0)),
            pl.BlockSpec(got.shape, lambda i: (0, 0, 0)),
            block,
        ],
        out_specs=block,
        scratch_shapes=[pltpu.VMEM((tiles, 3 * cells), BF16)],
        compiler_params=params(16),
        cost_estimate=cost(2 * tiles * fire * 3 * cells, 7 << 20),
        name="gradient",
    )(src, slot, got, burn)


def shifts(axis):
    count = lax.axis_size(axis)
    up = [(i, i + 1) for i in range(count - 1)]
    return up, [(j, i) for i, j in up]


def on_device(
    adjoint_forcing,
    courant_x,
    courant_y,
    vertical_mix,
    tile_block,
    injection_level,
    plume_profile,
    burn_weight,
):
    lev, nx, ny = adjoint_forcing.shape
    gx, gy = (lax.axis_size("gx"), lax.axis_size("gy"))
    procs = gx * gy
    tiles = injection_level.shape[0]
    sources = min(tiles // 4, procs // 2)
    cap = tiles // sources
    me = lax.axis_index(("gx", "gy"))
    me1 = me.astype(I32).reshape(1)
    fields = (adjoint_forcing, courant_x, courant_y, vertical_mix)

    fwd, back = shifts("gx")
    up, down = pack_x(*fields)
    above = lax.ppermute(down, "gx", fwd)
    below = lax.ppermute(up, "gx", back)
    edges = pack_y(*fields)
    own_l, send_l, own_r, send_r = pack_corner(above, below, edges)
    fwd, back = shifts("gy")
    got_l = lax.ppermute(send_r, "gy", fwd)
    got_r = lax.ppermute(send_l, "gy", back)

    levels_all = injection_level.reshape(1, tiles)
    for axis, count in (("gy", gy), ("gx", gx)):
        bit = 1
        while bit < count:
            pairs = [(i, i ^ bit) for i in range(count)]
            levels_all = jnp.concatenate([levels_all, lax.ppermute(levels_all, axis, pairs)], 0)
            bit *= 2

    row, shift, pos, src, slot = tile_indices(
        me1, tile_block.reshape(procs, tiles), cap, nx // TB, ny // TB, gy, nx
    )
    mid = stencil(*fields, above, below)
    state, columns = finish(
        me1, row, shift, pos, levels_all, plume_profile, mid, own_l, own_r, got_l, got_r, cap
    )
    columns = lax.all_to_all(columns, ("gx", "gy"), split_axis=0, concat_axis=0, tiled=True)
    return state, gradient(src, slot, columns, burn_weight)


def solution(mesh):
    return jax.shard_map(
        on_device,
        mesh=mesh,
        in_specs=(
            P(None, "gx", "gy"),
            P(None, "gx", "gy"),
            P(None, "gx", "gy"),
            P(None, "gx", "gy"),
            P(),
            P(("gx", "gy")),
            P(),
            P(("gx", "gy"), None),
        ),
        out_specs=(P(None, "gx", "gy"), P(("gx", "gy"), None)),
        check_vma=False,
    )
```

```python
import functools

import jax
import jax.numpy as jnp
from jax import lax
from jax.experimental import pallas as pl
from jax.experimental.pallas import tpu as pltpu
from jax.sharding import PartitionSpec as P

ITERS = 4
TB = 8
SUB = 100
LANES = 128
SUBL = 8
ROWS = 16
FRONT = 2 * SUBL
EDGE = SUBL
HALO = ITERS
UNROLL = 8

F32 = jnp.float32
BF16 = jnp.bfloat16
I32 = jnp.int32
ANY = pl.BlockSpec(memory_space=pl.ANY)
HBM = pl.BlockSpec(memory_space=pltpu.HBM)
VMEM = pl.BlockSpec(memory_space=pltpu.VMEM)
SMEM = pl.BlockSpec(memory_space=pltpu.SMEM)


def params(mib, **kw):
    return pltpu.CompilerParams(vmem_limit_bytes=mib << 20, **kw)


def cost(flops, nbytes):
    return pl.CostEstimate(flops=flops, bytes_accessed=nbytes, transcendentals=0)


def lane_id(shape):
    return lax.broadcasted_iota(I32, shape, 1)


def pack_x_kernel(vt, vb, cut, cub, cvt, cvb, kt, kb, up, dn):
    h, b = (HALO, ROWS)

    def level(l, _):
        up[0, l] = jnp.concatenate([vt[l, :h], cut[l].astype(F32)[:h]], 0)
        up[1, l] = jnp.concatenate([cvt[l].astype(F32)[:h], kt[l].astype(F32)[:h]], 0)
        dn[0, l] = jnp.concatenate([vb[l, SUBL - h :], cub[l].astype(F32)[b - h :]], 0)
        dn[1, l] = jnp.concatenate([cvb[l].astype(F32)[b - h :], kb[l].astype(F32)[b - h :]], 0)
        return 0

    lax.fori_loop(0, vt.shape[0], level, 0)


def pack_x(v, cu, cv, k):
    lev, nx, ny = v.shape

    def ends(x, rows):
        last = nx // rows - 1
        return (
            pl.BlockSpec((lev, rows, ny), lambda i: (0, 0, 0)),
            pl.BlockSpec((lev, rows, ny), lambda i: (0, last, 0)),
        )

    specs = [s for x, r in ((v, SUBL), (cu, ROWS), (cv, ROWS), (k, ROWS)) for s in ends(x, r)]
    out = jax.ShapeDtypeStruct((2, lev, 2 * HALO, ny), F32)
    whole = pl.BlockSpec((2, lev, 2 * HALO, ny), lambda i: (0, 0, 0, 0))
    return pl.pallas_call(
        pack_x_kernel,
        grid=(1,),
        out_shape=(out, out),
        in_specs=specs,
        out_specs=(whole, whole),
        compiler_params=params(12),
        cost_estimate=cost(0, 3 << 20),
        name="pack_x",
    )(v, v, cu, cu, cv, cv, k, k)


def edge_lanes(rows, lev, right):
    per = LANES // lev
    lane = lane_id((rows, LANES))
    take = lane // lev + (LANES - per if right else 0)
    return take, lane % lev


def pack_edge(slabs, take, level):
    acc = None
    for l, slab in enumerate(slabs):
        got = jnp.take_along_axis(slab, take, axis=1)
        acc = got if acc is None else jnp.where(level == l, got, acc)
    return acc


def store_edges(packed, own, send, at, right):
    v, cu, cv, k = packed
    for i, x in enumerate(packed):
        own[i, at, :] = x
    low = lane_id(v.shape) < LANES // 2
    half = LANES // 2
    for i, (a, b) in enumerate(((v, cu), (cv, k))):
        if right:
            send[i, at, :] = jnp.where(low, pltpu.roll(a, half, 1), b)
        else:
            send[i, at, :] = jnp.where(low, a, pltpu.roll(b, half, 1))


def load_group(ref, l, j, g, off=0):
    if off:
        return ref[l, j, pl.ds(g * SUBL + (FRONT - EDGE) + off, SUBL), :]
    return ref[l, j, pl.ds(pl.multiple_of(g * SUBL + (FRONT - EDGE), SUBL), SUBL), :]


def load_coef(ref, l, j, g):
    return ref[l, j, pl.ds(pl.multiple_of(g * SUBL, SUBL), SUBL), :]


def diffuse(get, mix, put, lev, nt):
    cur, below = (get(0), None)
    for l in range(lev):
        nxt = get(l + 1) if l + 1 < lev else None
        flux = []
        for j in range(nt):
            w = cur[j]
            if nxt is not None:
                f = mix(l, j) * (nxt[j] - cur[j])
                flux.append(f)
                w = w + (f - below[j]) if below else w + f
            elif below:
                w = w - below[j]
            put(l, j, w)
        cur, below = (nxt, flux)


def prepare_kernel(
    v_hbm, cu_hbm, cv_hbm, k_hbm, w, cuf, cvf, kf, own_l, send_l, own_r, send_r, vs, cus, cvs, ks, sem,
    *, lev, nx, nt, chunks,
):
    part = nx // chunks
    copies = []
    for c in range(chunks):
        at = pl.ds(c * part, part)
        pairs = ((v_hbm, vs), (k_hbm, ks), (cu_hbm, cus), (cv_hbm, cvs))
        copies.append(
            [
                pltpu.make_async_copy(src.at[:, at, :], dst.at[:, at, :], sem.at[c, i])
                for i, (src, dst) in enumerate(pairs)
            ]
        )
    for group in copies:
        for c in group:
            c.start()
    takes = [edge_lanes(ROWS, lev, side == 1) for side in range(2)]

    def rows(r, _):
        at = pl.ds(pl.multiple_of(r * ROWS, ROWS), ROWS)
        put = pl.ds(pl.multiple_of(r * ROWS + EDGE, SUBL), ROWS)
        here = pl.ds(pl.multiple_of(r * ROWS + FRONT, SUBL), ROWS)
        lanes = [slice(LANES * j, LANES * (j + 1)) for j in range(nt)]
        for l in range(lev):
            for j in range(nt):
                for buf, raw in ((cuf, cus), (cvf, cvs), (kf, ks)):
                    buf[l, j, put, :] = raw[l, at, lanes[j]].astype(F32)

        def store(l, j, x):
            w[l, j, here, :] = x

        diffuse(
            lambda l: [vs[l, at, lanes[j]] for j in range(nt)],
            lambda l, j: ks[l, at, lanes[j]].astype(F32),
            store,
            lev,
            nt,
        )
        for side, (own, send) in enumerate(((own_l, send_l), (own_r, send_r))):
            edge = lanes[-1] if side else lanes[0]
            packed = [
                pack_edge([x[l, at, edge].astype(F32) for l in range(lev)], *takes[side])
                for x in (vs, cus, cvs, ks)
            ]
            store_edges(packed, own, send, at, side == 1)
        return 0

    for c in range(chunks):
        for x in copies[c]:
            x.wait()
        lax.fori_loop(c * part // ROWS, (c + 1) * part // ROWS, rows, 0)


def prepare(v, cu, cv, k):
    lev, nx, ny = v.shape
    nt = ny // LANES
    chunks = max(c for c in (1, 2, 3, 4) if nx % (c * ROWS) == 0)
    wide = jax.ShapeDtypeStruct((lev, nt, nx + 2 * EDGE, LANES), F32)
    own = jax.ShapeDtypeStruct((4, nx + SUBL, LANES), F32)
    send = jax.ShapeDtypeStruct((2, nx + SUBL, LANES), F32)
    return pl.pallas_call(
        functools.partial(prepare_kernel, lev=lev, nx=nx, nt=nt, chunks=chunks),
        out_shape=(jax.ShapeDtypeStruct((lev, nt, nx + 2 * FRONT, LANES), F32), wide, wide, wide, own, send, own, send),
        in_specs=[HBM] * 4,
        out_specs=(VMEM,) * 8,
        scratch_shapes=[pltpu.VMEM((lev, nx, ny), F32)]
        + [pltpu.VMEM((lev, nx, ny), BF16)] * 3
        + [pltpu.SemaphoreType.DMA((chunks, 4))],
        compiler_params=params(14),
        cost_estimate=cost(20 * lev * nx * ny, 34 << 20),
        name="prepare",
    )(v, cu, cv, k)


def fill_kernel(above, below, *refs, lev, nx, nt):
    w, cuf, cvf, kf = refs[8:12]
    outs = refs[12:]
    rest = jnp.zeros((SUBL - HALO, LANES), F32)

    def pair(l, j, q, o):
        lanes = slice(LANES * j, LANES * (j + 1))
        top = jnp.concatenate([rest, above[q, l, o : o + HALO, lanes]], 0)
        return top, jnp.concatenate([below[q, l, o : o + HALO, lanes], rest], 0)

    for end in range(2):
        to = (FRONT + nx) if end else (FRONT - SUBL)
        at = (EDGE + nx) if end else (EDGE - SUBL)

        def store(l, j, x):
            w[l, j, to : to + SUBL, :] = x

        diffuse(
            lambda l: [pair(l, j, 0, 0)[end] for j in range(nt)],
            lambda l, j: pair(l, j, 1, HALO)[end],
            store,
            lev,
            nt,
        )
        for l in range(lev):
            for j in range(nt):
                for buf, q, o in ((cuf, 0, HALO), (cvf, 1, 0), (kf, 1, HALO)):
                    buf[l, j, at : at + SUBL, :] = pair(l, j, q, o)[end]
    for side in range(2):
        take, level = edge_lanes(SUBL, lev, side == 1)
        lanes = slice(LANES * (nt - 1), LANES * nt) if side else slice(0, LANES)
        packed = []
        for q, o in ((0, 0), (0, HALO), (1, 0), (1, HALO)):
            slabs = [
                jnp.concatenate([below[q, l, o : o + HALO, lanes], above[q, l, o : o + HALO, lanes]], 0)
                for l in range(lev)
            ]
            packed.append(pack_edge(slabs, take, level))
        store_edges(packed, outs[2 * side], outs[2 * side + 1], slice(nx, nx + SUBL), side == 1)


def fill(above, below, arrays):
    lev, _, _, ny = above.shape
    nt = ny // LANES
    nx = arrays[4].shape[1] - SUBL
    return pl.pallas_call(
        functools.partial(fill_kernel, lev=above.shape[1], nx=nx, nt=nt),
        out_shape=tuple(jax.ShapeDtypeStruct(x.shape, x.dtype) for x in arrays),
        in_specs=[VMEM] * 10,
        out_specs=(VMEM,) * 8,
        input_output_aliases={2 + i: i for i in range(8)},
        compiler_params=params(3),
        cost_estimate=cost(0, 4 << 20),
        name="fill",
    )(above, below, *arrays)


def sweep_kernel(src, cuf, cvf, *refs, lev, nx, nt, last_step):
    dst = refs[-1]
    lane = lane_id((SUBL, LANES))
    first, last = (lane == 0, lane == LANES - 1)

    def advect(l, g):
        mid = [load_group(src, l, j, g) for j in range(nt)]
        nxt = [pltpu.roll(x, LANES - 1, 1) for x in mid]
        prv = [pltpu.roll(x, 1, 1) for x in mid]
        out = []
        for j in range(nt):
            yp = jnp.where(last, nxt[j + 1], nxt[j]) if j + 1 < nt else nxt[j]
            ym = jnp.where(first, prv[j - 1], prv[j]) if j > 0 else prv[j]
            cu, cv = (load_coef(cuf, l, j, g), load_coef(cvf, l, j, g))
            wx = jnp.where(cu > 0, load_group(src, l, j, g, 1), load_group(src, l, j, g, -1))
            wy = jnp.where(cv > 0, yp, ym)
            out.append(mid[j] + jnp.abs(cu) * (wx - mid[j]) + jnp.abs(cv) * (wy - mid[j]))
        return out

    def body(g, _):
        if last_step:
            at = pl.ds(pl.multiple_of(g * SUBL - EDGE, SUBL), SUBL)
            for l in range(lev):
                for j, x in enumerate(advect(l, g)):
                    dst[l, j, at, :] = x
            return 0
        at = pl.ds(pl.multiple_of(g * SUBL + (FRONT - EDGE), SUBL), SUBL)

        def store(l, j, x):
            dst[l, j, at, :] = x

        diffuse(lambda l: advect(l, g), lambda l, j: load_coef(refs[0], l, j, g), store, lev, nt)
        return 0

    groups = nx // SUBL
    lo, hi = (1, groups + 1) if last_step else (0, groups + 2)
    whole = (hi - lo) // UNROLL

    def several(i, _):
        for n in range(UNROLL):
            body(lo + i * UNROLL + n, 0)
        return 0

    lax.fori_loop(0, whole, several, 0)
    for g in range(lo + whole * UNROLL, hi):
        body(g, 0)


def sweep(src, cuf, cvf, kf, last_step):
    lev, nt, rows, _ = src.shape
    nx = rows - 2 * FRONT
    ins = (src, cuf, cvf) if last_step else (src, cuf, cvf, kf)
    shape = (lev, nt, nx, LANES) if last_step else src.shape
    return pl.pallas_call(
        functools.partial(sweep_kernel, lev=lev, nx=nx, nt=nt, last_step=last_step),
        out_shape=jax.ShapeDtypeStruct(shape, F32),
        in_specs=[VMEM] * len(ins),
        out_specs=VMEM,
        compiler_params=params(3),
        cost_estimate=cost(18 * lev * nt * nx * LANES, 16 << 20),
        name="sweep_last" if last_step else "sweep",
    )(*ins)


def index_kernel(me_ref, blocks, row, shift, pos, src_col, slot_col, *, tiles, per_x, per_y, gy, cap, nx):
    per = tiles // LANES
    procs = blocks.shape[0] // per
    me = me_ref[0]
    per_tile = LANES // TB

    def lines(start, count, stride):
        return jnp.concatenate([blocks[pl.ds(start + i, count, stride), :] for i in range(per)], 1)

    def owner(b):
        br, bc = (b // (per_y * gy), b % (per_y * gy))
        return br // per_x * gy + bc // per_y, br % per_x, bc % per_y

    src, lr, lc = owner(lines(0, procs, per))
    mine = src == me
    t = lane_id((procs, tiles))
    upper = lax.broadcasted_iota(I32, (tiles, tiles), 0) <= lane_id((tiles, tiles))
    rank = jnp.dot(
        mine.astype(F32).astype(BF16), upper.astype(F32).astype(BF16), preferred_element_type=F32
    ).astype(I32)
    code = ((lc // per_tile * nx + lr * TB) * per_tile + lc % per_tile) * tiles + t + 1
    lane = lane_id((procs, LANES))
    found = jnp.zeros((procs, LANES), I32)
    for s in range(cap):
        hit = mine & (rank == s + 1)
        one = jnp.sum(jnp.where(hit, code, 0).astype(F32), axis=1, keepdims=True).astype(I32)
        found = jnp.where(lane == s, one, found)
    value = found - 1
    spot = value // tiles
    row[...] = jnp.where(found > 0, spot // per_tile, -1)
    shift[...] = (lane * TB - spot % per_tile * TB) & (LANES - 1)
    pos[...] = value % tiles
    own = owner(lines(me * per, 1, 1))[0]
    i = lax.broadcasted_iota(I32, (tiles, tiles), 0)
    j = lane_id((tiles, tiles))
    own_all = jnp.broadcast_to(own, (tiles, tiles)).astype(F32)
    col = jnp.sum(jnp.where(i == j, own_all, 0.0), axis=1, keepdims=True)
    same = (own_all == col) & (j < i)
    src_col[...] = col.astype(I32)
    slot_col[...] = jnp.sum(jnp.where(same, 1.0, 0.0), axis=1, keepdims=True).astype(I32)


def tile_indices(me, blocks, procs, cap, per_x, per_y, gy, nx):
    tiles = blocks.shape[0] // procs
    blocks = blocks.reshape(-1, LANES)
    table = jax.ShapeDtypeStruct((procs, LANES), I32)
    column = jax.ShapeDtypeStruct((tiles, 1), I32)
    return pl.pallas_call(
        functools.partial(index_kernel, tiles=tiles, per_x=per_x, per_y=per_y, gy=gy, cap=cap, nx=nx),
        out_shape=(table, table, table, column, column),
        in_specs=[SMEM, VMEM],
        out_specs=(VMEM,) * 5,
        compiler_params=params(8),
        cost_estimate=cost(0, 1 << 20),
        name="tile_indices",
    )(me, blocks)


def strips_kernel(own_l, own_r, got_l, got_r, out_l, out_r, strip, other, coef, *, lev, nx):
    rows = nx + 2 * HALO
    step = rows
    half = LANES // 2
    lane = lane_id((step, LANES))
    low = lane < half
    top_level = lane % lev == lev - 1
    head, tail = (lane < lev, lane >= LANES - lev)

    def turn(x):
        return pltpu.roll(x, half, 1)

    def gather(n, _):
        at = pl.ds(pl.multiple_of(n * step, SUBL), step)
        put = pl.ds(pl.multiple_of(n * step + SUBL, SUBL), step)
        for a in range(4):
            q = a // 2
            ol, orr = (own_l[a, at, :], own_r[a, at, :])
            gl, gr = (got_l[q, at, :], got_r[q, at, :])
            if a % 2:
                gl = turn(gl)
            else:
                gr = turn(gr)
            parts = (
                jnp.where(low, gl, turn(ol)),
                turn(jnp.where(low, orr, ol)),
                jnp.where(low, turn(orr), gr),
            )
            for i, x in enumerate(parts):
                if a == 0:
                    strip[i, put, :] = x
                elif a == 3:
                    coef[2, i, at, :] = jnp.where(top_level, 0.0, x)
                else:
                    coef[a - 1, i, at, :] = x
        return 0

    lax.fori_loop(0, rows // step, gather, 0)

    def diffuse(n, _):
        at = pl.ds(pl.multiple_of(n * step, SUBL), step)
        put = pl.ds(pl.multiple_of(n * step + SUBL, SUBL), step)
        for i in range(3):
            x = strip[i, put, :]
            f = coef[2, i, at, :] * (pltpu.roll(x, LANES - 1, 1) - x)
            other[i, put, :] = x + f - pltpu.roll(f, 1, 1)
        return 0

    def advect(n, _):
        at = pl.ds(pl.multiple_of(n * step, SUBL), step)
        put = pl.ds(pl.multiple_of(n * step + SUBL, SUBL), step)
        mid = [other[i, put, :] for i in range(3)]
        nxt = [pltpu.roll(x, LANES - lev, 1) for x in mid]
        prv = [pltpu.roll(x, lev, 1) for x in mid]
        yps = (jnp.where(tail, nxt[1], nxt[0]), jnp.where(tail, nxt[2], nxt[1]), nxt[2])
        yms = (prv[0], jnp.where(head, prv[0], prv[1]), jnp.where(head, prv[1], prv[2]))
        for i in range(3):
            cu, cv = (coef[0, i, at, :], coef[1, i, at, :])
            wx = jnp.where(
                cu > 0,
                other[i, pl.ds(n * step + SUBL + 1, step), :],
                other[i, pl.ds(n * step + SUBL - 1, step), :],
            )
            wy = jnp.where(cv > 0, yps[i], yms[i])
            strip[i, put, :] = mid[i] + jnp.abs(cu) * (wx - mid[i]) + jnp.abs(cv) * (wy - mid[i])
        return 0

    for _ in range(ITERS):
        lax.fori_loop(0, rows // step, diffuse, 0)
        for i in range(3):
            other[i, SUBL - 1 : SUBL, :] = other[i, SUBL + rows - 1 : SUBL + rows, :]
            other[i, SUBL + rows : SUBL + rows + 1, :] = other[i, SUBL : SUBL + 1, :]
        lax.fori_loop(0, rows // step, advect, 0)

    out_l[...] = strip[0, SUBL : SUBL + nx, :]
    out_r[...] = strip[2, SUBL : SUBL + nx, :]


def strips(own_l, own_r, got_l, got_r, lev):
    rows = own_l.shape[1]
    nx = rows - 2 * HALO
    out = jax.ShapeDtypeStruct((nx, LANES), F32)
    return pl.pallas_call(
        functools.partial(strips_kernel, lev=lev, nx=nx),
        out_shape=(out, out),
        in_specs=[VMEM] * 4,
        out_specs=(VMEM, VMEM),
        scratch_shapes=[
            pltpu.VMEM((3, rows + 2 * SUBL, LANES), F32),
            pltpu.VMEM((3, rows + 2 * SUBL, LANES), F32),
            pltpu.VMEM((3, 3, rows, LANES), F32),
        ],
        compiler_params=params(8),
        cost_estimate=cost(10 << 20, 3 << 20),
        name="strips",
    )(own_l, own_r, got_l, got_r)


def finish_kernel(
    me_ref, row, shift, pos, inj, prof, edge_l, edge_r, mid, state, send, field, weight, osem,
    *, lev, nx, nt, cap, procs, order,
):
    def spread(i, _):
        for l in range(lev):
            weight[i, l] = jnp.full((TB, LANES), prof[i, l], F32)
        return 0

    lax.fori_loop(0, lev, spread, 0)
    lane16 = lane_id((ROWS, LANES))
    width = HALO

    def patch(n, _):
        a = pl.ds(pl.multiple_of(n * ROWS, ROWS), ROWS)
        left, right = (edge_l[a, :], edge_r[a, :])
        for l in range(lev):
            take_l = (lane16 * lev + (LANES // 2 + l)) & (LANES - 1)
            take_r = ((lane16 - (LANES - width)) * lev + l) & (LANES - 1)
            b = pl.ds(pl.multiple_of((nt - 1) * nx + n * ROWS, ROWS), ROWS)
            field[l, a, :] = jnp.where(lane16 < width, jnp.take_along_axis(left, take_l, axis=1), field[l, a, :])
            field[l, b, :] = jnp.where(
                lane16 >= LANES - width, jnp.take_along_axis(right, take_r, axis=1), field[l, b, :]
            )
        return 0

    lax.fori_loop(0, nx // ROWS, patch, 0)
    puts = [
        pltpu.make_async_copy(
            field.at[:, pl.ds(j * nx, nx), :], state.at[:, :, pl.ds(j * LANES, LANES)], osem.at[j]
        )
        for j in range(nt)
    ]
    for c in puts:
        c.start()
    me = me_ref[0]
    slot_of = lane_id((TB, LANES)) // TB

    def handler(h, _):
        @pl.when(row[h, 0] >= 0)
        def _():
            out = jnp.zeros((TB, LANES), F32)
            apart = h ^ me
            source = 0
            for n, bit in enumerate(order):
                source = source + ((apart // bit) & 1) * (1 << n)
            for s in range(cap):
                at = pl.ds(pl.multiple_of(row[h, s], TB), TB)
                level = inj[source, pos[h, s]]
                terms = [weight[level, l] * field[l, at, :] for l in range(lev)]
                while len(terms) > 1:
                    terms = [x + y for x, y in zip(terms[::2], terms[1::2])]
                acc = terms[0]
                out = jnp.where(slot_of == s, pltpu.roll(acc, shift[h, s], 1), out)
            send[h] = out

        @pl.when(row[h, 0] < 0)
        def _():
            send[h] = jnp.zeros((TB, LANES), F32)

        return 0

    lax.fori_loop(0, procs, handler, 0)
    for c in puts:
        c.wait()


def finish(me, row, shift, pos, inj, prof, edge_l, edge_r, mid, cap, order):
    lev, nt, nx, _ = mid.shape
    procs = row.shape[0]
    mid = mid.reshape(lev, nt * nx, LANES)
    return pl.pallas_call(
        functools.partial(finish_kernel, lev=lev, nx=nx, nt=nt, cap=cap, procs=procs, order=order),
        out_shape=(
            jax.ShapeDtypeStruct((lev, nx, nt * LANES), F32),
            jax.ShapeDtypeStruct((procs, TB, LANES), F32),
            jax.ShapeDtypeStruct(mid.shape, F32),
        ),
        in_specs=[SMEM] * 6 + [VMEM] * 3,
        out_specs=(HBM, VMEM, VMEM),
        input_output_aliases={8: 2},
        scratch_shapes=[pltpu.VMEM((lev, lev, TB, LANES), F32), pltpu.SemaphoreType.DMA((nt,))],
        compiler_params=params(4),
        cost_estimate=cost(30 << 20, 20 << 20),
        name="finish",
    )(me, row, shift, pos, inj, prof, edge_l, edge_r, mid)


def split3(x):
    hi = x.astype(BF16)
    rest = x - hi.astype(F32)
    mid = rest.astype(BF16)
    return hi, mid, (rest - mid.astype(F32)).astype(BF16)


def gradient_kernel(src, slot, got, burn, out, cols, parts, *, cells):
    tiles, width = burn.shape
    procs = got.shape[0]
    step = pl.program_id(0)
    block = min(tiles, 8 * SUBL)

    @pl.when(step == 0)
    def _():
        for a in range(TB):
            parts[a] = jnp.concatenate(split3(got[:, a, :]), 0)
        lane = lane_id((block, LANES))
        low = lane < cells
        who = lane_id((block, 3 * procs)) % procs

        def rows(n, _):
            at = pl.ds(pl.multiple_of(n * block, block), block)
            pick = (who == src[at, :]).astype(F32).astype(BF16)
            keep = lane // TB == slot[at, :]
            t = [
                jnp.where(keep, jnp.dot(pick, parts[a], preferred_element_type=F32), 0.0)
                for a in range(TB)
            ]
            w = TB
            while len(t) > 1:
                even = lane & w == 0
                t = [
                    jnp.where(even, x, y) + pltpu.roll(jnp.where(even, y, x), w, 1)
                    for x, y in zip(t[::2], t[1::2])
                ]
                w *= 2
            col = t[0]
            while w < LANES:
                col = col + pltpu.roll(col, w, 1)
                w *= 2
            hi = col.astype(BF16).astype(F32)
            mid = (col - hi).astype(BF16).astype(F32)
            cols[at, :LANES] = jnp.where(low, hi, mid).astype(BF16)
            cols[at, LANES:] = jnp.where(low, col - hi - mid, 0.0).astype(BF16)
            return 0

        lax.fori_loop(0, tiles // block, rows, 0)

    q = step * width + lane_id((cells, width))
    c = lax.broadcasted_iota(I32, (cells, width), 0) * SUB
    spread = ((q >= c) & (q < c + SUB)).astype(F32).astype(BF16)
    wide = jnp.dot(
        cols[...], jnp.concatenate([spread] * (2 * LANES // cells), 0), preferred_element_type=F32
    )
    out[...] = (burn[...].astype(F32) * wide).astype(BF16)


def gradient(src, slot, got, burn):
    tiles, fire = burn.shape
    cells = TB * TB
    procs = got.shape[0]
    width = max(w for w in range(LANES, 11 * LANES, LANES) if fire % w == 0)
    block = pl.BlockSpec((tiles, width), lambda i: (0, i))
    return pl.pallas_call(
        functools.partial(gradient_kernel, cells=cells),
        grid=(fire // width,),
        out_shape=jax.ShapeDtypeStruct((tiles, fire), BF16),
        in_specs=[
            pl.BlockSpec((tiles, 1), lambda i: (0, 0)),
            pl.BlockSpec((tiles, 1), lambda i: (0, 0)),
            pl.BlockSpec(got.shape, lambda i: (0, 0, 0)),
            block,
        ],
        out_specs=block,
        scratch_shapes=[pltpu.VMEM((tiles, 2 * LANES), BF16), pltpu.VMEM((TB, 3 * procs, LANES), BF16)],
        compiler_params=params(16),
        cost_estimate=cost(2 * tiles * fire * 4 * cells, 7 << 20),
        name="gradient",
    )(src, slot, got, burn)


def shifts(axis):
    count = lax.axis_size(axis)
    up = [(i, i + 1) for i in range(count - 1)]
    return up, [(j, i) for i, j in up]


def bits(count):
    return [1 << n for n in range(count.bit_length() - 1)]


def on_device(
    adjoint_forcing,
    courant_x,
    courant_y,
    vertical_mix,
    tile_block,
    injection_level,
    plume_profile,
    burn_weight,
):
    lev, nx, ny = adjoint_forcing.shape
    gx, gy = (lax.axis_size("gx"), lax.axis_size("gy"))
    procs = gx * gy
    tiles = injection_level.shape[0]
    sources = min(tiles // 4, procs // 2)
    cap = tiles // sources
    me = lax.axis_index(("gx", "gy"))
    me1 = me.astype(I32).reshape(1)
    fields = tuple(
        pltpu.with_memory_space_constraint(x, pltpu.HBM)
        for x in (adjoint_forcing, courant_x, courant_y, vertical_mix)
    )

    steps = [("gx", b) for b in bits(gx)[::-1][:-1]] + [("gy", b) for b in bits(gy)[::-1]] + [("gx", 1)]
    order = tuple(b * gy if axis == "gx" else b for axis, b in steps)
    known = injection_level.reshape(1, tiles)

    def widen(known, step):
        axis, bit = step
        pairs = [(i, i ^ bit) for i in range(lax.axis_size(axis))]
        return jnp.concatenate([known, lax.ppermute(known, axis, pairs)], 0)

    up, down = pack_x(*fields)
    row, shift, pos, src, slot, up, down = lax.optimization_barrier(
        tuple(tile_indices(me1, tile_block, procs, cap, nx // TB, ny // TB, gy, nx)) + (up, down)
    )
    fwd, back = shifts("gx")
    above = lax.ppermute(down, "gx", fwd)
    below = lax.ppermute(up, "gx", back)
    arrays = fill(above, below, prepare(*fields))
    w, cu, cv, k, own_l, send_l, own_r, send_r = arrays
    fwd, back = shifts("gy")
    got_l = lax.ppermute(send_r, "gy", fwd)
    got_r = lax.ppermute(send_l, "gy", back)
    todo = list(steps)
    for n in range(ITERS):
        known, w = lax.optimization_barrier((known, w))
        share = len(todo[:-1]) // (ITERS - n) if n + 1 < ITERS else len(todo[:-1])
        for step in todo[:share]:
            known = widen(known, step)
        todo = todo[share:]
        w = sweep(w, cu, cv, k, n + 1 == ITERS)
    known, w, got_l, got_r = lax.optimization_barrier((known, w, got_l, got_r))
    for step in todo:
        known = widen(known, step)
    edge_l, edge_r = strips(own_l, own_r, got_l, got_r, lev)
    state, columns, _ = finish(
        me1, row, shift, pos, known, plume_profile, edge_l, edge_r, w, cap, order
    )
    columns = lax.all_to_all(columns, ("gx", "gy"), split_axis=0, concat_axis=0, tiled=True)
    return state, gradient(src, slot, columns, burn_weight)


def solution(mesh):
    return jax.shard_map(
        on_device,
        mesh=mesh,
        in_specs=(
            P(None, "gx", "gy"),
            P(None, "gx", "gy"),
            P(None, "gx", "gy"),
            P(None, "gx", "gy"),
            P(),
            P(("gx", "gy")),
            P(),
            P(("gx", "gy"), None),
        ),
        out_specs=(P(None, "gx", "gy"), P(("gx", "gy"), None)),
        check_vma=False,
    )
```

```python
import functools

import jax
import jax.numpy as jnp
from jax import lax
from jax.experimental import pallas as pl
from jax.experimental.pallas import tpu as pltpu
from jax.sharding import PartitionSpec as P

ITERS = 4
TB = 8
SUB = 100
LANES = 128
SUBL = 8
ROWS = 16
FRONT = 2 * SUBL
EDGE = SUBL
HALO = ITERS
UNROLL = 8

F32 = jnp.float32
BF16 = jnp.bfloat16
I32 = jnp.int32
ANY = pl.BlockSpec(memory_space=pl.ANY)
HBM = pl.BlockSpec(memory_space=pltpu.HBM)
VMEM = pl.BlockSpec(memory_space=pltpu.VMEM)
SMEM = pl.BlockSpec(memory_space=pltpu.SMEM)


def params(mib, **kw):
    return pltpu.CompilerParams(vmem_limit_bytes=mib << 20, **kw)


def cost(flops, nbytes):
    return pl.CostEstimate(flops=flops, bytes_accessed=nbytes, transcendentals=0)


def lane_id(shape):
    return lax.broadcasted_iota(I32, shape, 1)


def pack_x_kernel(odd, vt, vb, cut, cub, cvt, cvb, kt, kb, inj, near, far):
    h, b = (HALO, ROWS)
    lev = vt.shape[0]

    def pack(up, dn):
        def level(l, _):
            up[l] = jnp.concatenate([vt[l, :h], cut[l].astype(F32)[:h]], 0)
            up[lev + l] = jnp.concatenate([cvt[l].astype(F32)[:h], kt[l].astype(F32)[:h]], 0)
            dn[l] = jnp.concatenate([vb[l, SUBL - h :], cub[l].astype(F32)[b - h :]], 0)
            dn[lev + l] = jnp.concatenate([cvb[l].astype(F32)[b - h :], kb[l].astype(F32)[b - h :]], 0)
            return 0

        lax.fori_loop(0, lev, level, 0)

    @pl.when(odd[0] == 0)
    def _():
        pack(far, near)

    @pl.when(odd[0] != 0)
    def _():
        pack(near, far)

    near[2 * lev] = jnp.zeros(near.shape[1:], F32)
    near[2 * lev, : inj.shape[0], :LANES] = inj[...].astype(F32)


def pack_x(odd, v, cu, cv, k, inj):
    lev, nx, ny = v.shape

    def ends(x, rows):
        last = nx // rows - 1
        return (
            pl.BlockSpec((lev, rows, ny), lambda i: (0, 0, 0)),
            pl.BlockSpec((lev, rows, ny), lambda i: (0, last, 0)),
        )

    specs = [s for x, r in ((v, SUBL), (cu, ROWS), (cv, ROWS), (k, ROWS)) for s in ends(x, r)]
    near = (2 * lev + 1, 2 * HALO, ny)
    far = (2 * lev, 2 * HALO, ny)
    return pl.pallas_call(
        pack_x_kernel,
        grid=(1,),
        out_shape=(jax.ShapeDtypeStruct(near, F32), jax.ShapeDtypeStruct(far, F32)),
        in_specs=[SMEM] + specs + [pl.BlockSpec(inj.shape, lambda i: (0, 0))],
        out_specs=(pl.BlockSpec(near, lambda i: (0, 0, 0)), pl.BlockSpec(far, lambda i: (0, 0, 0))),
        compiler_params=params(12),
        cost_estimate=cost(0, 3 << 20),
        name="pack_x",
    )(odd, v, v, cu, cu, cv, cv, k, k, inj)


def edge_lanes(rows, lev, right):
    per = LANES // lev
    lane = lane_id((rows, LANES))
    take = lane // lev + (LANES - per if right else 0)
    return take, lane % lev


def pack_edge(slabs, take, level):
    acc = None
    for l, slab in enumerate(slabs):
        got = jnp.take_along_axis(slab, take, axis=1)
        acc = got if acc is None else jnp.where(level == l, got, acc)
    return acc


def store_edges(packed, owns, near, far, at, odd):
    half = LANES // 2
    low = lane_id(packed[0][0].shape) < half
    rows = owns[0].shape[1]
    for own, arrays in zip(owns, packed):
        for i, x in enumerate(arrays):
            own[i, at, :] = x
    for i in range(2):
        a, b = packed[0][2 * i : 2 * i + 2]
        left = jnp.where(low, a, pltpu.roll(b, half, 1))
        a, b = packed[1][2 * i : 2 * i + 2]
        right = jnp.where(low, pltpu.roll(a, half, 1), b)
        near[i, at, :] = jnp.where(odd, left, right)
        far[i, at, :] = jnp.where(odd, right, left)


def load_group(ref, l, j, g, off=0):
    if off:
        return ref[l, j, pl.ds(g * SUBL + (FRONT - EDGE) + off, SUBL), :]
    return ref[l, j, pl.ds(pl.multiple_of(g * SUBL + (FRONT - EDGE), SUBL), SUBL), :]


def load_coef(ref, l, j, g):
    return ref[l, j, pl.ds(pl.multiple_of(g * SUBL, SUBL), SUBL), :]


def diffuse(get, mix, put, lev, nt):
    cur, below = (get(0), None)
    for l in range(lev):
        nxt = get(l + 1) if l + 1 < lev else None
        flux = []
        for j in range(nt):
            w = cur[j]
            if nxt is not None:
                f = mix(l, j) * (nxt[j] - cur[j])
                flux.append(f)
                w = w + (f - below[j]) if below else w + f
            elif below:
                w = w - below[j]
            put(l, j, w)
        cur, below = (nxt, flux)


def prepare_kernel(
    odd_ref, v_hbm, cu_hbm, cv_hbm, k_hbm, w, cuf, cvf, kf, own_l, own_r, near, far, vs, cus, cvs, ks, sem,
    *, lev, nx, nt, chunks,
):
    part = nx // chunks
    copies = []
    for c in range(chunks):
        at = pl.ds(c * part, part)
        pairs = ((v_hbm, vs), (k_hbm, ks), (cu_hbm, cus), (cv_hbm, cvs))
        copies.append(
            [
                pltpu.make_async_copy(src.at[:, at, :], dst.at[:, at, :], sem.at[c, i])
                for i, (src, dst) in enumerate(pairs)
            ]
        )
    for group in copies:
        for c in group:
            c.start()
    takes = [edge_lanes(ROWS, lev, side == 1) for side in range(2)]

    def rows(r, _):
        at = pl.ds(pl.multiple_of(r * ROWS, ROWS), ROWS)
        put = pl.ds(pl.multiple_of(r * ROWS + EDGE, SUBL), ROWS)
        here = pl.ds(pl.multiple_of(r * ROWS + FRONT, SUBL), ROWS)
        lanes = [slice(LANES * j, LANES * (j + 1)) for j in range(nt)]
        raws = (vs, cus, cvs, ks)
        bufs = (None, cuf, cvf, kf)
        packed = [[None] * 4, [None] * 4]

        def store(l, j, x):
            w[l, j, here, :] = x
            for i in range(4):
                wide = raws[i][l, at, lanes[j]].astype(F32)
                if i:
                    bufs[i][l, j, put, :] = wide
                for side in range(2):
                    if j == (nt - 1) * side:
                        take, level = takes[side]
                        got = jnp.take_along_axis(wide, take, axis=1)
                        old = packed[side][i]
                        packed[side][i] = got if old is None else jnp.where(level == l, got, old)

        diffuse(
            lambda l: [vs[l, at, lanes[j]] for j in range(nt)],
            lambda l, j: ks[l, at, lanes[j]].astype(F32),
            store,
            lev,
            nt,
        )
        store_edges(packed, (own_l, own_r), near, far, at, odd_ref[0] != 0)
        return 0

    for c in range(chunks):
        for x in copies[c]:
            x.wait()
        lax.fori_loop(c * part // ROWS, (c + 1) * part // ROWS, rows, 0)


def prepare(odd, v, cu, cv, k):
    lev, nx, ny = v.shape
    nt = ny // LANES
    chunks = max(c for c in (1, 2, 3, 4) if nx % (c * ROWS) == 0)
    wide = jax.ShapeDtypeStruct((lev, nt, nx + 2 * EDGE, LANES), F32)
    own = jax.ShapeDtypeStruct((4, nx + SUBL, LANES), F32)
    near = jax.ShapeDtypeStruct((2, nx + 2 * SUBL, LANES), F32)
    far = jax.ShapeDtypeStruct((2, nx + SUBL, LANES), F32)
    return pl.pallas_call(
        functools.partial(prepare_kernel, lev=lev, nx=nx, nt=nt, chunks=chunks),
        out_shape=(jax.ShapeDtypeStruct((lev, nt, nx + 2 * FRONT, LANES), F32), wide, wide, wide, own, own, near, far),
        in_specs=[SMEM] + [HBM] * 4,
        out_specs=(VMEM,) * 8,
        scratch_shapes=[pltpu.VMEM((lev, nx, ny), F32)]
        + [pltpu.VMEM((lev, nx, ny), BF16)] * 3
        + [pltpu.SemaphoreType.DMA((chunks, 4))],
        compiler_params=params(14),
        cost_estimate=cost(20 * lev * nx * ny, 34 << 20),
        name="prepare",
    )(odd, v, cu, cv, k)


def fill_kernel(odd_x, odd_y, inj, got_near, got_far, *refs, lev, nx, nt):
    w, cuf, cvf, kf, own_l, own_r, near, far, known = refs[8:]
    rest = jnp.zeros((SUBL - HALO, LANES), F32)
    flip = odd_x[0] != 0

    def ends(l, j, q, o):
        at = (q * lev + l, slice(o, o + HALO), slice(LANES * j, LANES * (j + 1)))
        x, y = (got_near[at], got_far[at])
        return jnp.where(flip, x, y), jnp.where(flip, y, x)

    def pair(l, j, q, o):
        top, low = ends(l, j, q, o)
        return jnp.concatenate([rest, top], 0), jnp.concatenate([low, rest], 0)

    for end in range(2):
        to = (FRONT + nx) if end else (FRONT - SUBL)
        at = (EDGE + nx) if end else (EDGE - SUBL)

        def store(l, j, x):
            w[l, j, to : to + SUBL, :] = x

        diffuse(
            lambda l: [pair(l, j, 0, 0)[end] for j in range(nt)],
            lambda l, j: pair(l, j, 1, HALO)[end],
            store,
            lev,
            nt,
        )
        for l in range(lev):
            for j in range(nt):
                for buf, q, o in ((cuf, 0, HALO), (cvf, 1, 0), (kf, 1, HALO)):
                    buf[l, j, at : at + SUBL, :] = pair(l, j, q, o)[end]
    packed = []
    for side in range(2):
        take, level = edge_lanes(SUBL, lev, side == 1)
        packed.append([])
        for q, o in ((0, 0), (0, HALO), (1, 0), (1, HALO)):
            slabs = [jnp.concatenate(ends(l, (nt - 1) * side, q, o)[::-1], 0) for l in range(lev)]
            packed[-1].append(pack_edge(slabs, take, level))
    store_edges(packed, (own_l, own_r), near, far, slice(nx, nx + SUBL), odd_y[0] != 0)
    lines = inj.shape[0]
    tail = nx + SUBL
    known[:lines, :] = inj[...].astype(F32)
    known[lines:, :] = got_near[2 * lev, :lines, :LANES]
    for i in range(2):
        near[i, tail:, :] = jnp.zeros((SUBL, LANES), F32)
    near[0, tail : tail + 2 * lines, :] = known[...]


def fill(odd_x, odd_y, inj, got_near, got_far, arrays):
    lev = got_far.shape[0] // 2
    nt = got_far.shape[2] // LANES
    nx = arrays[4].shape[1] - SUBL
    known = jax.ShapeDtypeStruct((2 * inj.shape[0], LANES), F32)
    return pl.pallas_call(
        functools.partial(fill_kernel, lev=lev, nx=nx, nt=nt),
        out_shape=tuple(jax.ShapeDtypeStruct(x.shape, x.dtype) for x in arrays) + (known,),
        in_specs=[SMEM] * 2 + [VMEM] * 11,
        out_specs=(VMEM,) * 9,
        input_output_aliases={5 + i: i for i in range(8)},
        compiler_params=params(3),
        cost_estimate=cost(0, 4 << 20),
        name="fill",
    )(odd_x, odd_y, inj, got_near, got_far, *arrays)


def sweep_kernel(src, cuf, cvf, *refs, lev, nx, nt, last_step):
    dst = refs[-1]
    lane = lane_id((SUBL, LANES))
    first, last = (lane == 0, lane == LANES - 1)

    def advect(l, g):
        mid = [load_group(src, l, j, g) for j in range(nt)]
        nxt = [pltpu.roll(x, LANES - 1, 1) for x in mid]
        prv = [pltpu.roll(x, 1, 1) for x in mid]
        out = []
        for j in range(nt):
            yp = jnp.where(last, nxt[j + 1], nxt[j]) if j + 1 < nt else nxt[j]
            ym = jnp.where(first, prv[j - 1], prv[j]) if j > 0 else prv[j]
            cu, cv = (load_coef(cuf, l, j, g), load_coef(cvf, l, j, g))
            wx = jnp.where(cu > 0, load_group(src, l, j, g, 1), load_group(src, l, j, g, -1))
            wy = jnp.where(cv > 0, yp, ym)
            out.append(mid[j] + jnp.abs(cu) * (wx - mid[j]) + jnp.abs(cv) * (wy - mid[j]))
        return out

    def body(g, _):
        if last_step:
            at = pl.ds(pl.multiple_of(g * SUBL - EDGE, SUBL), SUBL)
            for l in range(lev):
                for j, x in enumerate(advect(l, g)):
                    dst[l, j, at, :] = x
            return 0
        at = pl.ds(pl.multiple_of(g * SUBL + (FRONT - EDGE), SUBL), SUBL)

        def store(l, j, x):
            dst[l, j, at, :] = x

        diffuse(lambda l: advect(l, g), lambda l, j: load_coef(refs[0], l, j, g), store, lev, nt)
        return 0

    groups = nx // SUBL
    lo, hi = (1, groups + 1) if last_step else (0, groups + 2)
    whole = (hi - lo) // UNROLL

    def several(i, _):
        for n in range(UNROLL):
            body(lo + i * UNROLL + n, 0)
        return 0

    lax.fori_loop(0, whole, several, 0)
    for g in range(lo + whole * UNROLL, hi):
        body(g, 0)


def sweep(src, cuf, cvf, kf, last_step):
    lev, nt, rows, _ = src.shape
    nx = rows - 2 * FRONT
    ins = (src, cuf, cvf) if last_step else (src, cuf, cvf, kf)
    shape = (lev, nt, nx, LANES) if last_step else src.shape
    return pl.pallas_call(
        functools.partial(sweep_kernel, lev=lev, nx=nx, nt=nt, last_step=last_step),
        out_shape=jax.ShapeDtypeStruct(shape, F32),
        in_specs=[VMEM] * len(ins),
        out_specs=VMEM,
        compiler_params=params(3),
        cost_estimate=cost(18 * lev * nt * nx * LANES, 16 << 20),
        name="sweep_last" if last_step else "sweep",
    )(*ins)


def index_kernel(me_ref, blocks, row, shift, pos, src_col, slot_col, *, tiles, per_x, per_y, gy, cap, nx):
    per = tiles // LANES
    procs = blocks.shape[0] // per
    me = me_ref[0]
    per_tile = LANES // TB

    def lines(start, count, stride):
        return jnp.concatenate([blocks[pl.ds(start + i, count, stride), :] for i in range(per)], 1)

    def owner(b):
        br, bc = (b // (per_y * gy), b % (per_y * gy))
        return br // per_x * gy + bc // per_y, br % per_x, bc % per_y

    src, lr, lc = owner(lines(0, procs, per))
    mine = src == me
    t = lane_id((procs, tiles))
    upper = lax.broadcasted_iota(I32, (tiles, tiles), 0) <= lane_id((tiles, tiles))
    rank = jnp.dot(
        mine.astype(F32).astype(BF16), upper.astype(F32).astype(BF16), preferred_element_type=F32
    ).astype(I32)
    code = ((lc // per_tile * nx + lr * TB) * per_tile + lc % per_tile) * tiles + t + 1
    lane = lane_id((procs, LANES))
    found = jnp.zeros((procs, LANES), I32)
    for s in range(cap):
        hit = mine & (rank == s + 1)
        one = jnp.sum(jnp.where(hit, code, 0).astype(F32), axis=1, keepdims=True).astype(I32)
        found = jnp.where(lane == s, one, found)
    value = found - 1
    spot = value // tiles
    row[...] = jnp.where(found > 0, spot // per_tile, 0)
    shift[...] = (lane * TB - spot % per_tile * TB) & (LANES - 1)
    pos[...] = jnp.where(found > 0, value % tiles, 0)
    own = owner(lines(me * per, 1, 1))[0]
    i = lax.broadcasted_iota(I32, (tiles, tiles), 0)
    j = lane_id((tiles, tiles))
    own_all = jnp.broadcast_to(own, (tiles, tiles)).astype(F32)
    col = jnp.sum(jnp.where(i == j, own_all, 0.0), axis=1, keepdims=True)
    same = (own_all == col) & (j < i)
    src_col[...] = col.astype(I32)
    slot_col[...] = jnp.sum(jnp.where(same, 1.0, 0.0), axis=1, keepdims=True).astype(I32)


def tile_indices(me, blocks, procs, cap, per_x, per_y, gy, nx):
    tiles = blocks.shape[0] // procs
    blocks = blocks.reshape(-1, LANES)
    table = jax.ShapeDtypeStruct((procs, LANES), I32)
    column = jax.ShapeDtypeStruct((tiles, 1), I32)
    return pl.pallas_call(
        functools.partial(index_kernel, tiles=tiles, per_x=per_x, per_y=per_y, gy=gy, cap=cap, nx=nx),
        out_shape=(table, table, table, column, column),
        in_specs=[SMEM, VMEM],
        out_specs=(VMEM,) * 5,
        compiler_params=params(8),
        cost_estimate=cost(0, 1 << 20),
        name="tile_indices",
    )(me, blocks)


def strips_kernel(odd, own_l, own_r, got_near, got_far, out_l, out_r, strip, other, coef, *, lev, nx):
    rows = nx + 2 * HALO
    step = rows
    half = LANES // 2
    lane = lane_id((step, LANES))
    low = lane < half
    top_level = lane % lev == lev - 1
    head, tail = (lane < lev, lane >= LANES - lev)

    def turn(x):
        return pltpu.roll(x, half, 1)

    def gather(n, _):
        at = pl.ds(pl.multiple_of(n * step, SUBL), step)
        put = pl.ds(pl.multiple_of(n * step + SUBL, SUBL), step)
        for a in range(4):
            q = a // 2
            ol, orr = (own_l[a, at, :], own_r[a, at, :])
            x, y = (got_near[q, at, :], got_far[q, at, :])
            gl, gr = (jnp.where(odd[0] != 0, x, y), jnp.where(odd[0] != 0, y, x))
            if a % 2:
                gl = turn(gl)
            else:
                gr = turn(gr)
            parts = (
                jnp.where(low, gl, turn(ol)),
                turn(jnp.where(low, orr, ol)),
                jnp.where(low, turn(orr), gr),
            )
            for i, x in enumerate(parts):
                if a == 0:
                    strip[i, put, :] = x
                elif a == 3:
                    coef[2, i, at, :] = jnp.where(top_level, 0.0, x)
                else:
                    coef[a - 1, i, at, :] = x
        return 0

    lax.fori_loop(0, rows // step, gather, 0)

    def diffuse(n, _):
        at = pl.ds(pl.multiple_of(n * step, SUBL), step)
        put = pl.ds(pl.multiple_of(n * step + SUBL, SUBL), step)
        for i in range(3):
            x = strip[i, put, :]
            f = coef[2, i, at, :] * (pltpu.roll(x, LANES - 1, 1) - x)
            other[i, put, :] = x + f - pltpu.roll(f, 1, 1)
        return 0

    def advect(n, _):
        at = pl.ds(pl.multiple_of(n * step, SUBL), step)
        put = pl.ds(pl.multiple_of(n * step + SUBL, SUBL), step)
        mid = [other[i, put, :] for i in range(3)]
        nxt = [pltpu.roll(x, LANES - lev, 1) for x in mid]
        prv = [pltpu.roll(x, lev, 1) for x in mid]
        yps = (jnp.where(tail, nxt[1], nxt[0]), jnp.where(tail, nxt[2], nxt[1]), nxt[2])
        yms = (prv[0], jnp.where(head, prv[0], prv[1]), jnp.where(head, prv[1], prv[2]))
        for i in range(3):
            cu, cv = (coef[0, i, at, :], coef[1, i, at, :])
            wx = jnp.where(
                cu > 0,
                other[i, pl.ds(n * step + SUBL + 1, step), :],
                other[i, pl.ds(n * step + SUBL - 1, step), :],
            )
            wy = jnp.where(cv > 0, yps[i], yms[i])
            strip[i, put, :] = mid[i] + jnp.abs(cu) * (wx - mid[i]) + jnp.abs(cv) * (wy - mid[i])
        return 0

    for _ in range(ITERS):
        lax.fori_loop(0, rows // step, diffuse, 0)
        for i in range(3):
            other[i, SUBL - 1 : SUBL, :] = other[i, SUBL + rows - 1 : SUBL + rows, :]
            other[i, SUBL + rows : SUBL + rows + 1, :] = other[i, SUBL : SUBL + 1, :]
        lax.fori_loop(0, rows // step, advect, 0)

    out_l[...] = strip[0, SUBL : SUBL + nx, :]
    out_r[...] = strip[2, SUBL : SUBL + nx, :]


def strips(odd, own_l, own_r, got_near, got_far, lev):
    rows = own_l.shape[1]
    nx = rows - 2 * HALO
    out = jax.ShapeDtypeStruct((nx, LANES), F32)
    return pl.pallas_call(
        functools.partial(strips_kernel, lev=lev, nx=nx),
        out_shape=(out, out),
        in_specs=[SMEM] + [VMEM] * 4,
        out_specs=(VMEM, VMEM),
        scratch_shapes=[
            pltpu.VMEM((3, rows + 2 * SUBL, LANES), F32),
            pltpu.VMEM((3, rows + 2 * SUBL, LANES), F32),
            pltpu.VMEM((3, 3, rows, LANES), F32),
        ],
        compiler_params=params(8),
        cost_estimate=cost(10 << 20, 3 << 20),
        name="strips",
    )(odd, own_l, own_r, got_near, got_far)


def finish_kernel(
    me_ref, row, shift, pos, inj, prof, edge_l, edge_r, mid, state, send, field, weight, osem,
    *, lev, nx, nt, cap, procs, order,
):
    def spread(i, _):
        for l in range(lev):
            weight[i, l] = jnp.full((TB, LANES), prof[i, l], F32)
        return 0

    lax.fori_loop(0, lev, spread, 0)
    lane8 = lane_id((SUBL, LANES))
    width = HALO
    outer, inner = (lane8 < width, lane8 >= LANES - width)
    base = (nt - 1) * nx

    def patch(n, _):
        for m in range(2):
            l = 2 * n + m
            take_l = (lane8 * lev + (LANES // 2 + l)) & (LANES - 1)
            take_r = ((lane8 - (LANES - width)) * lev + l) & (LANES - 1)
            for g in range(0, nx, SUBL):
                x, y = (edge_l[g : g + SUBL, :], edge_r[g : g + SUBL, :])
                x = jnp.take_along_axis(x, take_l, axis=1)
                field[l, g : g + SUBL, :] = jnp.where(outer, x, field[l, g : g + SUBL, :])
                y = jnp.take_along_axis(y, take_r, axis=1)
                g = base + g
                field[l, g : g + SUBL, :] = jnp.where(inner, y, field[l, g : g + SUBL, :])
        return 0

    lax.fori_loop(0, lev // 2, patch, 0)
    puts = [
        pltpu.make_async_copy(
            field.at[:, pl.ds(j * nx, nx), :], state.at[:, :, pl.ds(j * LANES, LANES)], osem.at[j]
        )
        for j in range(nt)
    ]
    for c in puts:
        c.start()
    me = me_ref[0]
    slot_of = lane_id((TB, LANES)) >> TB.bit_length() - 1

    def handler(h):
        out = jnp.zeros((TB, LANES), F32)
        apart = h ^ me
        source = 0
        lines = inj.shape[0] // procs
        for n, bit in enumerate(order):
            source = source | (apart >> bit.bit_length() - 1 & 1) << n
        for s in range(cap):
            at = pl.ds(pl.multiple_of(row[h, s], TB), TB)
            tile = pos[h, s]
            level = inj[source * lines + (tile >> LANES.bit_length() - 1), tile & (LANES - 1)]
            terms = [weight[level, l] * field[l, at, :] for l in range(lev)]
            while len(terms) > 1:
                terms = [x + y for x, y in zip(terms[::2], terms[1::2])]
            out = jnp.where(slot_of == s, pltpu.roll(terms[0], shift[h, s], 1), out)
        send[h] = out

    def handlers(n, _):
        for m in range(2):
            handler(2 * n + m)
        return 0

    lax.fori_loop(0, procs // 2, handlers, 0)
    for c in puts:
        c.wait()


def finish(me, row, shift, pos, inj, prof, edge_l, edge_r, mid, cap, order):
    lev, nt, nx, _ = mid.shape
    procs = row.shape[0]
    mid = mid.reshape(lev, nt * nx, LANES)
    return pl.pallas_call(
        functools.partial(finish_kernel, lev=lev, nx=nx, nt=nt, cap=cap, procs=procs, order=order),
        out_shape=(
            jax.ShapeDtypeStruct((lev, nx, nt * LANES), F32),
            jax.ShapeDtypeStruct((procs, TB, LANES), F32),
            jax.ShapeDtypeStruct(mid.shape, F32),
        ),
        in_specs=[SMEM] * 6 + [VMEM] * 3,
        out_specs=(HBM, VMEM, VMEM),
        input_output_aliases={8: 2},
        scratch_shapes=[pltpu.VMEM((lev, lev, TB, LANES), F32), pltpu.SemaphoreType.DMA((nt,))],
        compiler_params=params(4),
        cost_estimate=cost(30 << 20, 20 << 20),
        name="finish",
    )(me, row, shift, pos, inj, prof, edge_l, edge_r, mid)


def split3(x):
    hi = x.astype(BF16)
    rest = x - hi.astype(F32)
    mid = rest.astype(BF16)
    return hi, mid, (rest - mid.astype(F32)).astype(BF16)


def gradient_kernel(src, slot, got, burn, out, cols, parts, wide, sem, *, cells, width):
    tiles, fire = burn.shape
    procs = got.shape[0]
    block = min(tiles, 8 * SUBL)
    for a in range(TB):
        parts[a] = jnp.concatenate(split3(got[:, a, :]), 0)
    lane = lane_id((block, LANES))
    low = lane < cells
    which = lane >> TB.bit_length() - 1
    third = lane_id((block, 3 * procs))
    who = jnp.where(third >= procs, third - procs, third)
    who = jnp.where(who >= procs, who - procs, who)

    def rows(n, _):
        at = pl.ds(pl.multiple_of(n * block, block), block)
        pick = jnp.where(who == src[at, :], 1.0, 0.0).astype(BF16)
        keep = which == slot[at, :]
        t = [
            jnp.where(keep, jnp.dot(pick, parts[a], preferred_element_type=F32), 0.0)
            for a in range(TB)
        ]
        w = TB
        while len(t) > 1:
            even = lane & w == 0
            t = [
                jnp.where(even, x, y) + pltpu.roll(jnp.where(even, y, x), w, 1)
                for x, y in zip(t[::2], t[1::2])
            ]
            w *= 2
        col = t[0]
        while w < LANES:
            col = col + pltpu.roll(col, w, 1)
            w *= 2
        hi = col.astype(BF16).astype(F32)
        mid = (col - hi).astype(BF16).astype(F32)
        cols[at, :LANES] = jnp.where(low, hi, mid).astype(BF16)
        cols[at, LANES:] = jnp.where(low, col - hi - mid, 0.0).astype(BF16)
        return 0

    for n in range(tiles // block):
        rows(n, 0)
    c = lax.broadcasted_iota(I32, (cells, width), 0) * SUB
    lane = lane_id((cells, width)) - c
    copies = []
    for n in range(fire // width):
        q = lane + n * width
        spread = jnp.where((q >= 0) & (q < SUB), 1.0, 0.0).astype(BF16)
        at = slice(n * width, (n + 1) * width)
        full = jnp.dot(
            cols[...], jnp.concatenate([spread] * (2 * LANES // cells), 0), preferred_element_type=F32
        )
        wide[:, at] = (burn[:, at].astype(F32) * full).astype(BF16)
        copies.append(pltpu.make_async_copy(wide.at[:, at], out.at[:, at], sem.at[n]))
        copies[-1].start()
    for x in copies:
        x.wait()


def gradient(src, slot, got, burn):
    tiles, fire = burn.shape
    cells = TB * TB
    procs = got.shape[0]
    width = max(w for w in range(LANES, 11 * LANES, LANES) if fire % w == 0)
    return pl.pallas_call(
        functools.partial(gradient_kernel, cells=cells, width=width),
        out_shape=jax.ShapeDtypeStruct((tiles, fire), BF16),
        in_specs=[VMEM] * 4,
        out_specs=HBM,
        scratch_shapes=[
            pltpu.VMEM((tiles, 2 * LANES), BF16),
            pltpu.VMEM((TB, 3 * procs, LANES), BF16),
            pltpu.VMEM((tiles, fire), BF16),
            pltpu.SemaphoreType.DMA((fire // width,)),
        ],
        compiler_params=params(16),
        cost_estimate=cost(2 * tiles * fire * 4 * cells, 7 << 20),
        name="gradient",
    )(src, slot, got, burn)


def exchange(near, far, axis):
    count = lax.axis_size(axis)
    first = lax.ppermute(near, axis, [(i, i ^ 1) for i in range(count)])
    pairs = [(i, i + 1) for i in range(1, count - 1, 2)]
    return first, lax.ppermute(far, axis, pairs + [(j, i) for i, j in pairs])


def bits(count):
    return [1 << n for n in range(count.bit_length() - 1)]


def on_device(
    adjoint_forcing,
    courant_x,
    courant_y,
    vertical_mix,
    tile_block,
    injection_level,
    plume_profile,
    burn_weight,
):
    lev, nx, ny = adjoint_forcing.shape
    gx, gy = (lax.axis_size("gx"), lax.axis_size("gy"))
    procs = gx * gy
    tiles = injection_level.shape[0]
    sources = min(tiles // 4, procs // 2)
    cap = tiles // sources
    me = lax.axis_index(("gx", "gy"))
    me1 = me.astype(I32).reshape(1)
    fields = tuple(
        pltpu.with_memory_space_constraint(x, pltpu.HBM)
        for x in (adjoint_forcing, courant_x, courant_y, vertical_mix)
    )

    steps = [("gx", b) for b in bits(gx)[1:][::-1]] + [("gy", b) for b in bits(gy)[1:][::-1]]
    order = (gy, 1) + tuple(b * gy if axis == "gx" else b for axis, b in steps)
    inj = injection_level.reshape(-1, LANES)

    def widen(known, step):
        axis, bit = step
        pairs = [(i, i ^ bit) for i in range(lax.axis_size(axis))]
        return jnp.concatenate([known, lax.ppermute(known, axis, pairs)], 0)

    odd_x, odd_y = ((lax.axis_index(a).astype(I32) & 1).reshape(1) for a in ("gx", "gy"))
    near, far = pack_x(odd_x, *fields, inj)
    row, shift, pos, src, slot, near, far = lax.optimization_barrier(
        tuple(tile_indices(me1, tile_block, procs, cap, nx // TB, ny // TB, gy, nx)) + (near, far)
    )
    got_near, got_far = exchange(near, far, "gx")
    w, cu, cv, k, own_l, own_r, near, far, known = fill(
        odd_x, odd_y, inj, got_near, got_far, prepare(odd_y, *fields)
    )
    got_near, got_far = exchange(near, far, "gy")
    for n in range(ITERS):
        if n == ITERS // 2:
            w, got_near = lax.optimization_barrier((w, got_near))
            other = got_near[0, nx + SUBL : nx + SUBL + known.shape[0], :]
            known = jnp.concatenate([known, other], 0)
        if n >= ITERS // 2:
            known, w = lax.optimization_barrier((known, w))
            now = 1 if n + 1 < ITERS else len(steps) - 1
            for step in steps[:now]:
                known = widen(known, step)
            steps = steps[now:]
        w = sweep(w, cu, cv, k, n + 1 == ITERS)
    known, w = lax.optimization_barrier((known, w))
    for step in steps:
        known = widen(known, step)
    edge_l, edge_r = strips(odd_y, own_l, own_r, got_near, got_far, lev)
    state, columns, _ = finish(
        me1, row, shift, pos, known.astype(I32), plume_profile, edge_l, edge_r, w, cap, order
    )
    columns = lax.all_to_all(columns, ("gx", "gy"), split_axis=0, concat_axis=0, tiled=True)
    return state, gradient(src, slot, columns, burn_weight)


def solution(mesh):
    return jax.shard_map(
        on_device,
        mesh=mesh,
        in_specs=(
            P(None, "gx", "gy"),
            P(None, "gx", "gy"),
            P(None, "gx", "gy"),
            P(None, "gx", "gy"),
            P(),
            P(("gx", "gy")),
            P(),
            P(("gx", "gy"), None),
        ),
        out_specs=(P(None, "gx", "gy"), P(("gx", "gy"), None)),
        check_vma=False,
    )
```

```python
import functools

import jax
import jax.numpy as jnp
from jax import lax
from jax.experimental import pallas as pl
from jax.experimental.pallas import tpu as pltpu
from jax.sharding import PartitionSpec as P

ITERS = 4
TB = 8
SUB = 100
LANES = 128
SUBL = 8
ROWS = 16
FRONT = 2 * SUBL
EDGE = SUBL
HALO = ITERS
UNROLL = 8

F32 = jnp.float32
BF16 = jnp.bfloat16
I32 = jnp.int32
ANY = pl.BlockSpec(memory_space=pl.ANY)
HBM = pl.BlockSpec(memory_space=pltpu.HBM)
VMEM = pl.BlockSpec(memory_space=pltpu.VMEM)
SMEM = pl.BlockSpec(memory_space=pltpu.SMEM)


def params(mib, **kw):
    return pltpu.CompilerParams(vmem_limit_bytes=mib << 20, **kw)


def cost(flops, nbytes):
    return pl.CostEstimate(flops=flops, bytes_accessed=nbytes, transcendentals=0)


def lane_id(shape):
    return lax.broadcasted_iota(I32, shape, 1)


def pack_x_kernel(odd, vt, vb, cut, cub, cvt, cvb, kt, kb, inj, near, far):
    h, b = (HALO, ROWS)
    lev = vt.shape[0]

    def pack(up, dn):
        def level(l, _):
            up[l] = jnp.concatenate([vt[l, :h], cut[l].astype(F32)[:h]], 0)
            up[lev + l] = jnp.concatenate([cvt[l].astype(F32)[:h], kt[l].astype(F32)[:h]], 0)
            dn[l] = jnp.concatenate([vb[l, SUBL - h :], cub[l].astype(F32)[b - h :]], 0)
            dn[lev + l] = jnp.concatenate([cvb[l].astype(F32)[b - h :], kb[l].astype(F32)[b - h :]], 0)
            return 0

        lax.fori_loop(0, lev, level, 0)

    @pl.when(odd[0] == 0)
    def _():
        pack(far, near)

    @pl.when(odd[0] != 0)
    def _():
        pack(near, far)

    near[2 * lev] = jnp.zeros(near.shape[1:], F32)
    near[2 * lev, : inj.shape[0], :LANES] = inj[...].astype(F32)


def pack_x(odd, v, cu, cv, k, inj):
    lev, nx, ny = v.shape

    def ends(x, rows):
        last = nx // rows - 1
        return (
            pl.BlockSpec((lev, rows, ny), lambda i: (0, 0, 0)),
            pl.BlockSpec((lev, rows, ny), lambda i: (0, last, 0)),
        )

    specs = [s for x, r in ((v, SUBL), (cu, ROWS), (cv, ROWS), (k, ROWS)) for s in ends(x, r)]
    near = (2 * lev + 1, 2 * HALO, ny)
    far = (2 * lev, 2 * HALO, ny)
    return pl.pallas_call(
        pack_x_kernel,
        grid=(1,),
        out_shape=(jax.ShapeDtypeStruct(near, F32), jax.ShapeDtypeStruct(far, F32)),
        in_specs=[SMEM] + specs + [pl.BlockSpec(inj.shape, lambda i: (0, 0))],
        out_specs=(pl.BlockSpec(near, lambda i: (0, 0, 0)), pl.BlockSpec(far, lambda i: (0, 0, 0))),
        compiler_params=params(12),
        cost_estimate=cost(0, 3 << 20),
        name="pack_x",
    )(odd, v, v, cu, cu, cv, cv, k, k, inj)


def edge_lanes(rows, lev, right):
    per = LANES // lev
    lane = lane_id((rows, LANES))
    take = lane // lev + (LANES - per if right else 0)
    return take, lane % lev


def pack_edge(slabs, take, level):
    acc = None
    for l, slab in enumerate(slabs):
        got = jnp.take_along_axis(slab, take, axis=1)
        acc = got if acc is None else jnp.where(level == l, got, acc)
    return acc


def store_edges(packed, owns, near, far, at, odd):
    half = LANES // 2
    low = lane_id(packed[0][0].shape) < half
    rows = owns[0].shape[1]
    for own, arrays in zip(owns, packed):
        for i, x in enumerate(arrays):
            own[i, at, :] = x
    for i in range(2):
        a, b = packed[0][2 * i : 2 * i + 2]
        left = jnp.where(low, a, pltpu.roll(b, half, 1))
        a, b = packed[1][2 * i : 2 * i + 2]
        right = jnp.where(low, pltpu.roll(a, half, 1), b)
        near[i, at, :] = jnp.where(odd, left, right)
        far[i, at, :] = jnp.where(odd, right, left)


def load_group(ref, l, j, g, off=0):
    if off:
        return ref[l, j, pl.ds(g * SUBL + (FRONT - EDGE) + off, SUBL), :]
    return ref[l, j, pl.ds(pl.multiple_of(g * SUBL + (FRONT - EDGE), SUBL), SUBL), :]


def load_coef(ref, l, j, g):
    return ref[l, j, pl.ds(pl.multiple_of(g * SUBL, SUBL), SUBL), :]


def diffuse(get, mix, put, lev, nt):
    cur, below = (get(0), None)
    for l in range(lev):
        nxt = get(l + 1) if l + 1 < lev else None
        flux = []
        for j in range(nt):
            w = cur[j]
            if nxt is not None:
                f = mix(l, j) * (nxt[j] - cur[j])
                flux.append(f)
                w = w + (f - below[j]) if below else w + f
            elif below:
                w = w - below[j]
            put(l, j, w)
        cur, below = (nxt, flux)


def index_kernel(me_ref, blocks, row, shift, pos, src_col, slot_col, *, tiles, per_x, per_y, gy, cap, nx):
    per = tiles // LANES
    procs = blocks.shape[0] // per
    me = me_ref[0]
    per_tile = LANES // TB

    def lines(start, count, stride):
        return jnp.concatenate([blocks[pl.ds(start + i, count, stride), :] for i in range(per)], 1)

    def owner(b):
        br, bc = (b // (per_y * gy), b % (per_y * gy))
        return br // per_x * gy + bc // per_y, br % per_x, bc % per_y

    src, lr, lc = owner(lines(0, procs, per))
    mine = src == me
    t = lane_id((procs, tiles))
    upper = lax.broadcasted_iota(I32, (tiles, tiles), 0) <= lane_id((tiles, tiles))
    rank = jnp.dot(
        mine.astype(F32).astype(BF16), upper.astype(F32).astype(BF16), preferred_element_type=F32
    ).astype(I32)
    code = ((lc // per_tile * (nx // TB) + lr) * per_tile + lc % per_tile) * tiles + t + 1
    lane = lane_id((procs, LANES))
    found = jnp.zeros((procs, LANES), I32)
    for s in range(cap):
        hit = mine & (rank == s + 1)
        one = jnp.sum(jnp.where(hit, code, 0).astype(F32), axis=1, keepdims=True).astype(I32)
        found = jnp.where(lane == s, one, found)
    value = found - 1
    spot = value // tiles
    row[...] = jnp.where(found > 0, spot // per_tile, 0)
    shift[...] = (lane * TB - spot % per_tile * TB) & (LANES - 1)
    pos[...] = jnp.where(found > 0, value % tiles, 0)
    own = owner(lines(me * per, 1, 1))[0]
    i = lax.broadcasted_iota(I32, (tiles, tiles), 0)
    j = lane_id((tiles, tiles))
    own_all = jnp.broadcast_to(own, (tiles, tiles)).astype(F32)
    col = jnp.sum(jnp.where(i == j, own_all, 0.0), axis=1, keepdims=True)
    same = (own_all == col) & (j < i)
    src_col[...] = col.astype(I32)
    slot_col[...] = jnp.sum(jnp.where(same, 1.0, 0.0), axis=1, keepdims=True).astype(I32)


def prepare_kernel(
    odd_ref, me_ref, blocks_hbm, v_hbm, cu_hbm, cv_hbm, k_hbm, w, cuf, cvf, kf, own_l, own_r, near, far,
    row, shift, pos, src_col, slot_col, vs, cus, cvs, ks, blocks, sem, bsem, *, lev, nx, nt, chunks, index,
):
    table = pltpu.make_async_copy(blocks_hbm, blocks, bsem)
    table.start()
    part = nx // chunks
    copies = []
    for c in range(chunks):
        at = pl.ds(c * part, part)
        pairs = ((v_hbm, vs), (k_hbm, ks), (cu_hbm, cus), (cv_hbm, cvs))
        copies.append(
            [
                pltpu.make_async_copy(src.at[:, at, :], dst.at[:, at, :], sem.at[c, i])
                for i, (src, dst) in enumerate(pairs)
            ]
        )
    for group in copies:
        for c in group:
            c.start()
    takes = [edge_lanes(ROWS, lev, side == 1) for side in range(2)]

    def rows(r, _):
        at = pl.ds(pl.multiple_of(r * ROWS, ROWS), ROWS)
        put = pl.ds(pl.multiple_of(r * ROWS + EDGE, SUBL), ROWS)
        here = pl.ds(pl.multiple_of(r * ROWS + FRONT, SUBL), ROWS)
        lanes = [slice(LANES * j, LANES * (j + 1)) for j in range(nt)]
        raws = (vs, cus, cvs, ks)
        bufs = (None, cuf, cvf, kf)
        packed = [[None] * 4, [None] * 4]

        def store(l, j, x):
            w[l, j, here, :] = x
            for i in range(4):
                wide = raws[i][l, at, lanes[j]].astype(F32)
                if i:
                    bufs[i][l, j, put, :] = wide
                for side in range(2):
                    if j == (nt - 1) * side:
                        take, level = takes[side]
                        got = jnp.take_along_axis(wide, take, axis=1)
                        old = packed[side][i]
                        packed[side][i] = got if old is None else jnp.where(level == l, got, old)

        diffuse(
            lambda l: [vs[l, at, lanes[j]] for j in range(nt)],
            lambda l, j: ks[l, at, lanes[j]].astype(F32),
            store,
            lev,
            nt,
        )
        store_edges(packed, (own_l, own_r), near, far, at, odd_ref[0] != 0)
        return 0

    def two(n, _):
        rows(2 * n, 0)
        return rows(2 * n + 1, 0)

    for c in range(chunks):
        for x in copies[c]:
            x.wait()
        lax.fori_loop(c * part // ROWS, (c + 1) * part // ROWS, rows, 0)

    table.wait()
    index_kernel(me_ref, blocks, row, shift, pos, src_col, slot_col, nx=nx, **index)


def prepare(odd, me, tile_block, procs, cap, gy, v, cu, cv, k):
    lev, nx, ny = v.shape
    nt = ny // LANES
    chunks = max(c for c in (1, 2, 3, 4) if nx % (c * ROWS) == 0)
    tiles = tile_block.shape[0] // procs
    blocks = pltpu.with_memory_space_constraint(tile_block.reshape(-1, LANES), pltpu.HBM)
    index = dict(tiles=tiles, per_x=nx // TB, per_y=ny // TB, gy=gy, cap=cap)
    table = jax.ShapeDtypeStruct((procs, LANES), I32)
    column = jax.ShapeDtypeStruct((tiles, 1), I32)
    wide = jax.ShapeDtypeStruct((lev, nt, nx + 2 * EDGE, LANES), F32)
    own = jax.ShapeDtypeStruct((4, nx + SUBL, LANES), F32)
    near = jax.ShapeDtypeStruct((2, nx + 2 * SUBL, LANES), F32)
    far = jax.ShapeDtypeStruct((2, nx + SUBL, LANES), F32)
    return pl.pallas_call(
        functools.partial(prepare_kernel, lev=lev, nx=nx, nt=nt, chunks=chunks, index=index),
        out_shape=(jax.ShapeDtypeStruct((lev, nt, nx + 2 * FRONT, LANES), F32), wide, wide, wide, own, own, near, far)
        + (table,) * 3
        + (column,) * 2,
        in_specs=[SMEM] * 2 + [HBM] * 5,
        out_specs=(VMEM,) * 13,
        scratch_shapes=[pltpu.VMEM((lev, nx, ny), F32)]
        + [pltpu.VMEM((lev, nx, ny), BF16)] * 3
        + [pltpu.VMEM(blocks.shape, I32), pltpu.SemaphoreType.DMA((chunks, 4)), pltpu.SemaphoreType.DMA],
        compiler_params=params(14),
        cost_estimate=cost(20 * lev * nx * ny, 34 << 20),
        name="prepare",
    )(odd, me, blocks, v, cu, cv, k)


def fill_kernel(odd_x, odd_y, inj, got_near, got_far, *refs, lev, nx, nt):
    w, cuf, cvf, kf, own_l, own_r, near, far, known = refs[8:]
    rest = jnp.zeros((SUBL - HALO, LANES), F32)
    flip = odd_x[0] != 0

    def ends(l, j, q, o):
        at = (q * lev + l, slice(o, o + HALO), slice(LANES * j, LANES * (j + 1)))
        x, y = (got_near[at], got_far[at])
        return jnp.where(flip, x, y), jnp.where(flip, y, x)

    def pair(l, j, q, o):
        top, low = ends(l, j, q, o)
        return jnp.concatenate([rest, top], 0), jnp.concatenate([low, rest], 0)

    for end in range(2):
        to = (FRONT + nx) if end else (FRONT - SUBL)
        at = (EDGE + nx) if end else (EDGE - SUBL)

        def store(l, j, x):
            w[l, j, to : to + SUBL, :] = x

        diffuse(
            lambda l: [pair(l, j, 0, 0)[end] for j in range(nt)],
            lambda l, j: pair(l, j, 1, HALO)[end],
            store,
            lev,
            nt,
        )
        for l in range(lev):
            for j in range(nt):
                for buf, q, o in ((cuf, 0, HALO), (cvf, 1, 0), (kf, 1, HALO)):
                    buf[l, j, at : at + SUBL, :] = pair(l, j, q, o)[end]
    packed = []
    for side in range(2):
        take, level = edge_lanes(SUBL, lev, side == 1)
        packed.append([])
        for q, o in ((0, 0), (0, HALO), (1, 0), (1, HALO)):
            slabs = [jnp.concatenate(ends(l, (nt - 1) * side, q, o)[::-1], 0) for l in range(lev)]
            packed[-1].append(pack_edge(slabs, take, level))
    store_edges(packed, (own_l, own_r), near, far, slice(nx, nx + SUBL), odd_y[0] != 0)
    lines = inj.shape[0]
    tail = nx + SUBL
    known[:lines, :] = inj[...].astype(F32)
    known[lines:, :] = got_near[2 * lev, :lines, :LANES]
    for i in range(2):
        near[i, tail:, :] = jnp.zeros((SUBL, LANES), F32)
    near[0, tail : tail + 2 * lines, :] = known[...]


def fill(odd_x, odd_y, inj, got_near, got_far, arrays):
    lev = got_far.shape[0] // 2
    nt = got_far.shape[2] // LANES
    nx = arrays[4].shape[1] - SUBL
    known = jax.ShapeDtypeStruct((2 * inj.shape[0], LANES), F32)
    return pl.pallas_call(
        functools.partial(fill_kernel, lev=lev, nx=nx, nt=nt),
        out_shape=tuple(jax.ShapeDtypeStruct(x.shape, x.dtype) for x in arrays) + (known,),
        in_specs=[SMEM] * 2 + [VMEM] * 11,
        out_specs=(VMEM,) * 9,
        input_output_aliases={5 + i: i for i in range(8)},
        compiler_params=params(3),
        cost_estimate=cost(0, 4 << 20),
        name="fill",
    )(odd_x, odd_y, inj, got_near, got_far, *arrays)


def sweep_kernel(src, cuf, cvf, *refs, lev, nx, nt, last_step):
    dst = refs[-1]
    lane = lane_id((SUBL, LANES))
    first, last = (lane == 0, lane == LANES - 1)

    def advect(l, g):
        mid = [load_group(src, l, j, g) for j in range(nt)]
        nxt = [pltpu.roll(x, LANES - 1, 1) for x in mid]
        prv = [pltpu.roll(x, 1, 1) for x in mid]
        out = []
        for j in range(nt):
            yp = jnp.where(last, nxt[j + 1], nxt[j]) if j + 1 < nt else nxt[j]
            ym = jnp.where(first, prv[j - 1], prv[j]) if j > 0 else prv[j]
            cu, cv = (load_coef(cuf, l, j, g), load_coef(cvf, l, j, g))
            wx = jnp.where(cu > 0, load_group(src, l, j, g, 1), load_group(src, l, j, g, -1))
            wy = jnp.where(cv > 0, yp, ym)
            out.append(mid[j] + jnp.abs(cu) * (wx - mid[j]) + jnp.abs(cv) * (wy - mid[j]))
        return out

    def body(g, _):
        if last_step:
            for l in range(lev):
                for j, x in enumerate(advect(l, g)):
                    dst[j * (nx // SUBL) + g - 1, l] = x
            return 0
        at = pl.ds(pl.multiple_of(g * SUBL + (FRONT - EDGE), SUBL), SUBL)

        def store(l, j, x):
            dst[l, j, at, :] = x

        diffuse(lambda l: advect(l, g), lambda l, j: load_coef(refs[0], l, j, g), store, lev, nt)
        return 0

    groups = nx // SUBL
    lo, hi = (1, groups + 1) if last_step else (0, groups + 2)
    whole = (hi - lo) // UNROLL

    def several(i, _):
        for n in range(UNROLL):
            body(lo + i * UNROLL + n, 0)
        return 0

    lax.fori_loop(0, whole, several, 0)
    for g in range(lo + whole * UNROLL, hi):
        body(g, 0)


def sweep(src, cuf, cvf, kf, last_step):
    lev, nt, rows, _ = src.shape
    nx = rows - 2 * FRONT
    ins = (src, cuf, cvf) if last_step else (src, cuf, cvf, kf)
    shape = (nt * nx // SUBL, lev, SUBL, LANES) if last_step else src.shape
    return pl.pallas_call(
        functools.partial(sweep_kernel, lev=lev, nx=nx, nt=nt, last_step=last_step),
        out_shape=jax.ShapeDtypeStruct(shape, F32),
        in_specs=[VMEM] * len(ins),
        out_specs=VMEM,
        compiler_params=params(3),
        cost_estimate=cost(18 * lev * nt * nx * LANES, 16 << 20),
        name="sweep_last" if last_step else "sweep",
    )(*ins)


def strips_kernel(odd, own_l, own_r, got_near, got_far, out_l, out_r, strip, other, coef, *, lev, nx):
    rows = nx + 2 * HALO
    step = rows
    half = LANES // 2
    lane = lane_id((step, LANES))
    low = lane < half
    top_level = lane % lev == lev - 1
    head, tail = (lane < lev, lane >= LANES - lev)

    def turn(x):
        return pltpu.roll(x, half, 1)

    def gather(n, _):
        at = pl.ds(pl.multiple_of(n * step, SUBL), step)
        put = pl.ds(pl.multiple_of(n * step + SUBL, SUBL), step)
        for a in range(4):
            q = a // 2
            ol, orr = (own_l[a, at, :], own_r[a, at, :])
            x, y = (got_near[q, at, :], got_far[q, at, :])
            gl, gr = (jnp.where(odd[0] != 0, x, y), jnp.where(odd[0] != 0, y, x))
            if a % 2:
                gl = turn(gl)
            else:
                gr = turn(gr)
            parts = (
                jnp.where(low, gl, turn(ol)),
                turn(jnp.where(low, orr, ol)),
                jnp.where(low, turn(orr), gr),
            )
            for i, x in enumerate(parts):
                if a == 0:
                    strip[i, put, :] = x
                elif a == 3:
                    coef[2, i, at, :] = jnp.where(top_level, 0.0, x)
                else:
                    coef[a - 1, i, at, :] = x
        return 0

    lax.fori_loop(0, rows // step, gather, 0)

    def diffuse(n, _):
        at = pl.ds(pl.multiple_of(n * step, SUBL), step)
        put = pl.ds(pl.multiple_of(n * step + SUBL, SUBL), step)
        for i in range(3):
            x = strip[i, put, :]
            f = coef[2, i, at, :] * (pltpu.roll(x, LANES - 1, 1) - x)
            other[i, put, :] = x + f - pltpu.roll(f, 1, 1)
        return 0

    def advect(n, _):
        at = pl.ds(pl.multiple_of(n * step, SUBL), step)
        put = pl.ds(pl.multiple_of(n * step + SUBL, SUBL), step)
        mid = [other[i, put, :] for i in range(3)]
        nxt = [pltpu.roll(x, LANES - lev, 1) for x in mid]
        prv = [pltpu.roll(x, lev, 1) for x in mid]
        yps = (jnp.where(tail, nxt[1], nxt[0]), jnp.where(tail, nxt[2], nxt[1]), nxt[2])
        yms = (prv[0], jnp.where(head, prv[0], prv[1]), jnp.where(head, prv[1], prv[2]))
        for i in range(3):
            cu, cv = (coef[0, i, at, :], coef[1, i, at, :])
            wx = jnp.where(
                cu > 0,
                other[i, pl.ds(n * step + SUBL + 1, step), :],
                other[i, pl.ds(n * step + SUBL - 1, step), :],
            )
            wy = jnp.where(cv > 0, yps[i], yms[i])
            strip[i, put, :] = mid[i] + jnp.abs(cu) * (wx - mid[i]) + jnp.abs(cv) * (wy - mid[i])
        return 0

    for _ in range(ITERS):
        lax.fori_loop(0, rows // step, diffuse, 0)
        for i in range(3):
            other[i, SUBL - 1 : SUBL, :] = other[i, SUBL + rows - 1 : SUBL + rows, :]
            other[i, SUBL + rows : SUBL + rows + 1, :] = other[i, SUBL : SUBL + 1, :]
        lax.fori_loop(0, rows // step, advect, 0)

    out_l[...] = strip[0, SUBL : SUBL + nx, :]
    out_r[...] = strip[2, SUBL : SUBL + nx, :]


def strips(odd, own_l, own_r, got_near, got_far, lev):
    rows = own_l.shape[1]
    nx = rows - 2 * HALO
    out = jax.ShapeDtypeStruct((nx, LANES), F32)
    return pl.pallas_call(
        functools.partial(strips_kernel, lev=lev, nx=nx),
        out_shape=(out, out),
        in_specs=[SMEM] + [VMEM] * 4,
        out_specs=(VMEM, VMEM),
        scratch_shapes=[
            pltpu.VMEM((3, rows + 2 * SUBL, LANES), F32),
            pltpu.VMEM((3, rows + 2 * SUBL, LANES), F32),
            pltpu.VMEM((3, 3, rows, LANES), F32),
        ],
        compiler_params=params(8),
        cost_estimate=cost(10 << 20, 3 << 20),
        name="strips",
    )(odd, own_l, own_r, got_near, got_far)


def finish_kernel(
    me_ref, row, shift, pos, inj, prof, edge_l, edge_r, mid, state, send, field, weight, osem,
    *, lev, nx, nt, cap, procs, order,
):
    def spread(i, _):
        for l in range(lev):
            weight[i, l] = jnp.full((TB, LANES), prof[i, l], F32)
        return 0

    lax.fori_loop(0, lev, spread, 0)
    lane8 = lane_id((SUBL, LANES))
    width = HALO
    outer, inner = (lane8 < width, lane8 >= LANES - width)
    base = (nt - 1) * nx // SUBL

    def patch(n, _):
        for m in range(2):
            l = 2 * n + m
            take_l = (lane8 * lev + (LANES // 2 + l)) & (LANES - 1)
            take_r = ((lane8 - (LANES - width)) * lev + l) & (LANES - 1)
            for g in range(0, nx, SUBL):
                x, y = (edge_l[g : g + SUBL, :], edge_r[g : g + SUBL, :])
                x = jnp.take_along_axis(x, take_l, axis=1)
                y = jnp.take_along_axis(y, take_r, axis=1)
                g //= SUBL
                field[g, l] = jnp.where(outer, x, field[g, l])
                g += base
                field[g, l] = jnp.where(inner, y, field[g, l])
        return 0

    lax.fori_loop(0, lev // 2, patch, 0)
    count = nx // SUBL
    puts = [
        pltpu.make_async_copy(
            field.at[pl.ds(j * count, count), l],
            state.at[l, :, :, pl.ds(j * LANES, LANES)],
            osem.at[j, l],
        )
        for j in range(nt)
        for l in range(lev)
    ]
    for c in puts:
        c.start()
    me = me_ref[0]
    slot_of = lane_id((TB, LANES)) >> TB.bit_length() - 1

    def handler(h):
        out = jnp.zeros((TB, LANES), F32)
        apart = h ^ me
        source = 0
        lines = inj.shape[0] // procs
        for n, bit in enumerate(order):
            source = source | (apart >> bit.bit_length() - 1 & 1) << n
        for s in range(cap):
            at = row[h, s]
            tile = pos[h, s]
            level = inj[source * lines + (tile >> LANES.bit_length() - 1), tile & (LANES - 1)]
            terms = [weight[level, l] * field[at, l] for l in range(lev)]
            while len(terms) > 1:
                terms = [x + y for x, y in zip(terms[::2], terms[1::2])]
            out = jnp.where(slot_of == s, pltpu.roll(terms[0], shift[h, s], 1), out)
        send[h] = out

    def handlers(n, _):
        for m in range(2):
            handler(2 * n + m)
        return 0

    lax.fori_loop(0, procs // 2, handlers, 0)
    for c in puts:
        c.wait()


def finish(me, row, shift, pos, inj, prof, edge_l, edge_r, mid, cap, order):
    lev, nx = (mid.shape[1], edge_l.shape[0])
    nt = mid.shape[0] * SUBL // nx
    procs = row.shape[0]
    state, send, _ = pl.pallas_call(
        functools.partial(finish_kernel, lev=lev, nx=nx, nt=nt, cap=cap, procs=procs, order=order),
        out_shape=(
            jax.ShapeDtypeStruct((lev, nx // SUBL, SUBL, nt * LANES), F32),
            jax.ShapeDtypeStruct((procs, TB, LANES), F32),
            jax.ShapeDtypeStruct(mid.shape, F32),
        ),
        in_specs=[SMEM] * 6 + [VMEM] * 3,
        out_specs=(HBM, VMEM, VMEM),
        input_output_aliases={8: 2},
        scratch_shapes=[pltpu.VMEM((lev, lev, TB, LANES), F32), pltpu.SemaphoreType.DMA((nt, lev))],
        compiler_params=params(4),
        cost_estimate=cost(30 << 20, 20 << 20),
        name="finish",
    )(me, row, shift, pos, inj, prof, edge_l, edge_r, mid)
    return state.reshape(lev, nx, nt * LANES), send


def split3(x):
    hi = x.astype(BF16)
    rest = x - hi.astype(F32)
    mid = rest.astype(BF16)
    return hi, mid, (rest - mid.astype(F32)).astype(BF16)


def gradient_kernel(src, slot, got, burn, out, cols, parts, wide, sem, *, cells, width):
    tiles, fire = burn.shape
    procs = got.shape[0]
    block = min(tiles, 8 * SUBL)
    for a in range(TB):
        parts[a] = jnp.concatenate(split3(got[:, a, :]), 0)
    lane = lane_id((block, LANES))
    low = lane < cells
    which = lane >> TB.bit_length() - 1
    third = lane_id((block, 3 * procs))
    who = jnp.where(third >= procs, third - procs, third)
    who = jnp.where(who >= procs, who - procs, who)

    def rows(n, _):
        at = pl.ds(pl.multiple_of(n * block, block), block)
        pick = jnp.where(who == src[at, :], 1.0, 0.0).astype(BF16)
        keep = which == slot[at, :]
        t = [
            jnp.where(keep, jnp.dot(pick, parts[a], preferred_element_type=F32), 0.0)
            for a in range(TB)
        ]
        w = TB
        while len(t) > 1:
            even = lane & w == 0
            t = [
                jnp.where(even, x, y) + pltpu.roll(jnp.where(even, y, x), w, 1)
                for x, y in zip(t[::2], t[1::2])
            ]
            w *= 2
        col = t[0]
        while w < LANES:
            col = col + pltpu.roll(col, w, 1)
            w *= 2
        hi = col.astype(BF16).astype(F32)
        mid = (col - hi).astype(BF16).astype(F32)
        cols[at, :LANES] = jnp.where(low, hi, mid).astype(BF16)
        cols[at, LANES:] = jnp.where(low, col - hi - mid, 0.0).astype(BF16)
        return 0

    for n in range(tiles // block):
        rows(n, 0)
    c = lax.broadcasted_iota(I32, (cells, width), 0) * SUB
    lane = lane_id((cells, width)) - c
    copies = []
    for n in range(fire // width):
        q = lane + n * width
        spread = jnp.where((q >= 0) & (q < SUB), 1.0, 0.0).astype(BF16)
        at = slice(n * width, (n + 1) * width)
        full = jnp.dot(
            cols[...], jnp.concatenate([spread] * (2 * LANES // cells), 0), preferred_element_type=F32
        )
        wide[:, at] = (burn[:, at].astype(F32) * full).astype(BF16)
        copies.append(pltpu.make_async_copy(wide.at[:, at], out.at[:, at], sem.at[n]))
        copies[-1].start()
    for x in copies:
        x.wait()


def gradient(src, slot, got, burn):
    tiles, fire = burn.shape
    cells = TB * TB
    procs = got.shape[0]
    width = max(w for w in range(LANES, 11 * LANES, LANES) if fire % w == 0)
    return pl.pallas_call(
        functools.partial(gradient_kernel, cells=cells, width=width),
        out_shape=jax.ShapeDtypeStruct((tiles, fire), BF16),
        in_specs=[VMEM] * 4,
        out_specs=HBM,
        scratch_shapes=[
            pltpu.VMEM((tiles, 2 * LANES), BF16),
            pltpu.VMEM((TB, 3 * procs, LANES), BF16),
            pltpu.VMEM((tiles, fire), BF16),
            pltpu.SemaphoreType.DMA((fire // width,)),
        ],
        compiler_params=params(16),
        cost_estimate=cost(2 * tiles * fire * 4 * cells, 7 << 20),
        name="gradient",
    )(src, slot, got, burn)


def exchange(near, far, axis):
    count = lax.axis_size(axis)
    first = lax.ppermute(near, axis, [(i, i ^ 1) for i in range(count)])
    pairs = [(i, i + 1) for i in range(1, count - 1, 2)]
    return first, lax.ppermute(far, axis, pairs + [(j, i) for i, j in pairs])


def bits(count):
    return [1 << n for n in range(count.bit_length() - 1)]


def on_device(
    adjoint_forcing,
    courant_x,
    courant_y,
    vertical_mix,
    tile_block,
    injection_level,
    plume_profile,
    burn_weight,
):
    lev, nx, ny = adjoint_forcing.shape
    gx, gy = (lax.axis_size("gx"), lax.axis_size("gy"))
    procs = gx * gy
    tiles = injection_level.shape[0]
    sources = min(tiles // 4, procs // 2)
    cap = tiles // sources
    me = lax.axis_index(("gx", "gy"))
    me1 = me.astype(I32).reshape(1)
    fields = tuple(
        pltpu.with_memory_space_constraint(x, pltpu.HBM)
        for x in (adjoint_forcing, courant_x, courant_y, vertical_mix)
    )

    steps = [("gx", b) for b in bits(gx)[1:][::-1]] + [("gy", b) for b in bits(gy)[1:][::-1]]
    order = (gy, 1) + tuple(b * gy if axis == "gx" else b for axis, b in steps)
    inj = injection_level.reshape(-1, LANES)

    def widen(known, step):
        axis, bit = step
        pairs = [(i, i ^ bit) for i in range(lax.axis_size(axis))]
        return jnp.concatenate([known, lax.ppermute(known, axis, pairs)], 0)

    odd_x, odd_y = ((lax.axis_index(a).astype(I32) & 1).reshape(1) for a in ("gx", "gy"))
    near, far = pack_x(odd_x, *fields, pltpu.with_memory_space_constraint(inj, pltpu.HBM))
    got_near, got_far = exchange(near, far, "gx")
    ready = prepare(odd_y, me1, tile_block, procs, cap, gy, *fields)
    row, shift, pos, src, slot = ready[8:]
    w, cu, cv, k, own_l, own_r, near, far, known = fill(odd_x, odd_y, inj, got_near, got_far, ready[:8])
    got_near, got_far = exchange(near, far, "gy")
    for n in range(ITERS):
        if n == ITERS // 2:
            w, got_near = lax.optimization_barrier((w, got_near))
            other = got_near[0, nx + SUBL : nx + SUBL + known.shape[0], :]
            known = jnp.concatenate([known, other], 0)
        if n >= ITERS // 2:
            known, w = lax.optimization_barrier((known, w))
            now = 1 if n + 1 < ITERS else len(steps) - 1
            for step in steps[:now]:
                known = widen(known, step)
            steps = steps[now:]
        w = sweep(w, cu, cv, k, n + 1 == ITERS)
    known, w = lax.optimization_barrier((known, w))
    for step in steps:
        known = widen(known, step)
    edge_l, edge_r = strips(odd_y, own_l, own_r, got_near, got_far, lev)
    state, columns = finish(
        me1, row, shift, pos, known.astype(I32), plume_profile, edge_l, edge_r, w, cap, order
    )
    columns = lax.all_to_all(columns, ("gx", "gy"), split_axis=0, concat_axis=0, tiled=True)
    return state, gradient(src, slot, columns, burn_weight)


def solution(mesh):
    return jax.shard_map(
        on_device,
        mesh=mesh,
        in_specs=(
            P(None, "gx", "gy"),
            P(None, "gx", "gy"),
            P(None, "gx", "gy"),
            P(None, "gx", "gy"),
            P(),
            P(("gx", "gy")),
            P(),
            P(("gx", "gy"), None),
        ),
        out_specs=(P(None, "gx", "gy"), P(("gx", "gy"), None)),
        check_vma=False,
    )
```

```python
import functools

import jax
import jax.numpy as jnp
from jax import lax
from jax.experimental import pallas as pl
from jax.experimental.pallas import tpu as pltpu
from jax.sharding import PartitionSpec as P

ITERS = 4
TB = 8
SUB = 100
LANES = 128
SUBL = 8
ROWS = 16
FRONT = 2 * SUBL
EDGE = SUBL
HALO = ITERS
UNROLL = 8

F32 = jnp.float32
BF16 = jnp.bfloat16
I32 = jnp.int32
ANY = pl.BlockSpec(memory_space=pl.ANY)
HBM = pl.BlockSpec(memory_space=pltpu.HBM)
VMEM = pl.BlockSpec(memory_space=pltpu.VMEM)
SMEM = pl.BlockSpec(memory_space=pltpu.SMEM)


def params(mib, **kw):
    return pltpu.CompilerParams(vmem_limit_bytes=mib << 20, **kw)


def cost(flops, nbytes):
    return pl.CostEstimate(flops=flops, bytes_accessed=nbytes, transcendentals=0)


def lane_id(shape):
    return lax.broadcasted_iota(I32, shape, 1)


def pack_x_kernel(odd, vt, vb, cut, cub, cvt, cvb, kt, kb, inj, near, far):
    h, b = (HALO, ROWS)
    lev = vt.shape[0]

    def pack(up, dn):
        def level(l, _):
            up[l] = jnp.concatenate([vt[l, :h], cut[l].astype(F32)[:h]], 0)
            up[lev + l] = jnp.concatenate([cvt[l].astype(F32)[:h], kt[l].astype(F32)[:h]], 0)
            dn[l] = jnp.concatenate([vb[l, SUBL - h :], cub[l].astype(F32)[b - h :]], 0)
            dn[lev + l] = jnp.concatenate([cvb[l].astype(F32)[b - h :], kb[l].astype(F32)[b - h :]], 0)
            return 0

        lax.fori_loop(0, lev, level, 0)

    @pl.when(odd[0] == 0)
    def _():
        pack(far, near)

    @pl.when(odd[0] != 0)
    def _():
        pack(near, far)

    near[2 * lev] = jnp.zeros(near.shape[1:], F32)
    near[2 * lev, : inj.shape[0], :LANES] = inj[...].astype(F32)


def pack_x(odd, v, cu, cv, k, inj):
    lev, nx, ny = v.shape

    def ends(x, rows):
        last = nx // rows - 1
        return (
            pl.BlockSpec((lev, rows, ny), lambda i: (0, 0, 0)),
            pl.BlockSpec((lev, rows, ny), lambda i: (0, last, 0)),
        )

    specs = [s for x, r in ((v, SUBL), (cu, ROWS), (cv, ROWS), (k, ROWS)) for s in ends(x, r)]
    near = (2 * lev + 1, 2 * HALO, ny)
    far = (2 * lev, 2 * HALO, ny)
    return pl.pallas_call(
        pack_x_kernel,
        grid=(1,),
        out_shape=(jax.ShapeDtypeStruct(near, F32), jax.ShapeDtypeStruct(far, F32)),
        in_specs=[SMEM] + specs + [pl.BlockSpec(inj.shape, lambda i: (0, 0))],
        out_specs=(pl.BlockSpec(near, lambda i: (0, 0, 0)), pl.BlockSpec(far, lambda i: (0, 0, 0))),
        compiler_params=params(12),
        cost_estimate=cost(0, 3 << 20),
        name="pack_x",
    )(odd, v, v, cu, cu, cv, cv, k, k, inj)


def edge_lanes(rows, lev, right):
    per = LANES // lev
    lane = lane_id((rows, LANES))
    take = lane // lev + (LANES - per if right else 0)
    return take, lane % lev


def pack_edge(slabs, take, level):
    acc = None
    for l, slab in enumerate(slabs):
        got = jnp.take_along_axis(slab, take, axis=1)
        acc = got if acc is None else jnp.where(level == l, got, acc)
    return acc


def store_edges(packed, owns, near, far, at, odd):
    half = LANES // 2
    low = lane_id(packed[0][0].shape) < half
    rows = owns[0].shape[1]
    for own, arrays in zip(owns, packed):
        for i, x in enumerate(arrays):
            own[i, at, :] = x
    for i in range(2):
        a, b = packed[0][2 * i : 2 * i + 2]
        left = jnp.where(low, a, pltpu.roll(b, half, 1))
        a, b = packed[1][2 * i : 2 * i + 2]
        right = jnp.where(low, pltpu.roll(a, half, 1), b)
        near[i, at, :] = jnp.where(odd, left, right)
        far[i, at, :] = jnp.where(odd, right, left)


def load_group(ref, l, j, g, off=0):
    if off:
        return ref[l, j, pl.ds(g * SUBL + (FRONT - EDGE) + off, SUBL), :]
    return ref[l, j, pl.ds(pl.multiple_of(g * SUBL + (FRONT - EDGE), SUBL), SUBL), :]


def load_coef(ref, l, j, g):
    return ref[l, j, pl.ds(pl.multiple_of(g * SUBL, SUBL), SUBL), :]


def diffuse(get, mix, put, lev, nt):
    cur, below = (get(0), None)
    for l in range(lev):
        nxt = get(l + 1) if l + 1 < lev else None
        flux = []
        for j in range(nt):
            w = cur[j]
            if nxt is not None:
                f = mix(l, j) * (nxt[j] - cur[j])
                flux.append(f)
                w = w + (f - below[j]) if below else w + f
            elif below:
                w = w - below[j]
            put(l, j, w)
        cur, below = (nxt, flux)


def index_kernel(me_ref, blocks, row, shift, pos, src_col, slot_col, *, tiles, per_x, per_y, gy, cap, nx):
    per = tiles // LANES
    procs = blocks.shape[0] // per
    me = me_ref[0]
    per_tile = LANES // TB

    def lines(start, count, stride):
        return jnp.concatenate([blocks[pl.ds(start + i, count, stride), :] for i in range(per)], 1)

    def owner(b):
        br, bc = (b // (per_y * gy), b % (per_y * gy))
        return br // per_x * gy + bc // per_y, br % per_x, bc % per_y

    src, lr, lc = owner(lines(0, procs, per))
    mine = src == me
    t = lane_id((procs, tiles))
    upper = lax.broadcasted_iota(I32, (tiles, tiles), 0) <= lane_id((tiles, tiles))
    rank = jnp.dot(
        mine.astype(F32).astype(BF16), upper.astype(F32).astype(BF16), preferred_element_type=F32
    ).astype(I32)
    code = ((lc // per_tile * (nx // TB) + lr) * per_tile + lc % per_tile) * tiles + t + 1
    lane = lane_id((procs, LANES))
    found = jnp.zeros((procs, LANES), I32)
    for s in range(cap):
        hit = mine & (rank == s + 1)
        one = jnp.sum(jnp.where(hit, code, 0).astype(F32), axis=1, keepdims=True).astype(I32)
        found = jnp.where(lane == s, one, found)
    value = found - 1
    spot = value // tiles
    row[...] = jnp.where(found > 0, spot // per_tile, 0)
    shift[...] = (lane * TB - spot % per_tile * TB) & (LANES - 1)
    pos[...] = jnp.where(found > 0, value % tiles, 0)
    own = owner(lines(me * per, 1, 1))[0]
    i = lax.broadcasted_iota(I32, (tiles, tiles), 0)
    j = lane_id((tiles, tiles))
    own_all = jnp.broadcast_to(own, (tiles, tiles)).astype(F32)
    col = jnp.sum(jnp.where(i == j, own_all, 0.0), axis=1, keepdims=True)
    same = (own_all == col) & (j < i)
    src_col[...] = col.astype(I32)
    slot_col[...] = jnp.sum(jnp.where(same, 1.0, 0.0), axis=1, keepdims=True).astype(I32)


def prepare_kernel(
    odd_ref, me_ref, blocks_hbm, v_hbm, cu_hbm, cv_hbm, k_hbm, w, cuf, cvf, kf, own_l, own_r, near, far,
    row, shift, pos, src_col, slot_col, vs, cus, cvs, ks, blocks, sem, bsem, *, lev, nx, nt, chunks, index,
):
    table = pltpu.make_async_copy(blocks_hbm, blocks, bsem)
    table.start()
    part = nx // chunks
    copies = []
    for c in range(chunks):
        at = pl.ds(c * part, part)
        pairs = ((v_hbm, vs), (k_hbm, ks), (cu_hbm, cus), (cv_hbm, cvs))
        copies.append(
            [
                pltpu.make_async_copy(src.at[:, at, :], dst.at[:, at, :], sem.at[c, i])
                for i, (src, dst) in enumerate(pairs)
            ]
        )
    for group in copies:
        for c in group:
            c.start()
    takes = [edge_lanes(ROWS, lev, side == 1) for side in range(2)]

    def rows(r, _):
        at = pl.ds(pl.multiple_of(r * ROWS, ROWS), ROWS)
        put = pl.ds(pl.multiple_of(r * ROWS + EDGE, SUBL), ROWS)
        here = pl.ds(pl.multiple_of(r * ROWS + FRONT, SUBL), ROWS)
        lanes = [slice(LANES * j, LANES * (j + 1)) for j in range(nt)]
        raws = (vs, cus, cvs, ks)
        bufs = (None, cuf, cvf, kf)
        packed = [[None] * 4, [None] * 4]

        def store(l, j, x):
            w[l, j, here, :] = x
            for i in range(4):
                wide = raws[i][l, at, lanes[j]].astype(F32)
                if i:
                    bufs[i][l, j, put, :] = wide
                for side in range(2):
                    if j == (nt - 1) * side:
                        take, level = takes[side]
                        got = jnp.take_along_axis(wide, take, axis=1)
                        old = packed[side][i]
                        packed[side][i] = got if old is None else jnp.where(level == l, got, old)

        diffuse(
            lambda l: [vs[l, at, lanes[j]] for j in range(nt)],
            lambda l, j: ks[l, at, lanes[j]].astype(F32),
            store,
            lev,
            nt,
        )
        store_edges(packed, (own_l, own_r), near, far, at, odd_ref[0] != 0)
        return 0

    def two(n, _):
        rows(2 * n, 0)
        return rows(2 * n + 1, 0)

    for c in range(chunks):
        for x in copies[c]:
            x.wait()
        lax.fori_loop(c * part // ROWS, (c + 1) * part // ROWS, rows, 0)

    table.wait()
    index_kernel(me_ref, blocks, row, shift, pos, src_col, slot_col, nx=nx, **index)


def prepare(odd, me, tile_block, procs, cap, gy, v, cu, cv, k):
    lev, nx, ny = v.shape
    nt = ny // LANES
    chunks = max(c for c in (1, 2, 3, 4) if nx % (c * ROWS) == 0)
    tiles = tile_block.shape[0] // procs
    blocks = pltpu.with_memory_space_constraint(tile_block.reshape(-1, LANES), pltpu.HBM)
    index = dict(tiles=tiles, per_x=nx // TB, per_y=ny // TB, gy=gy, cap=cap)
    table = jax.ShapeDtypeStruct((procs, LANES), I32)
    column = jax.ShapeDtypeStruct((tiles, 1), I32)
    wide = jax.ShapeDtypeStruct((lev, nt, nx + 2 * EDGE, LANES), F32)
    own = jax.ShapeDtypeStruct((4, nx + SUBL, LANES), F32)
    near = jax.ShapeDtypeStruct((2, nx + 2 * SUBL, LANES), F32)
    far = jax.ShapeDtypeStruct((2, nx + SUBL, LANES), F32)
    return pl.pallas_call(
        functools.partial(prepare_kernel, lev=lev, nx=nx, nt=nt, chunks=chunks, index=index),
        out_shape=(jax.ShapeDtypeStruct((lev, nt, nx + 2 * FRONT, LANES), F32), wide, wide, wide, own, own, near, far)
        + (table,) * 3
        + (column,) * 2,
        in_specs=[SMEM] * 2 + [HBM] * 5,
        out_specs=(VMEM,) * 13,
        scratch_shapes=[pltpu.VMEM((lev, nx, ny), F32)]
        + [pltpu.VMEM((lev, nx, ny), BF16)] * 3
        + [pltpu.VMEM(blocks.shape, I32), pltpu.SemaphoreType.DMA((chunks, 4)), pltpu.SemaphoreType.DMA],
        compiler_params=params(14),
        cost_estimate=cost(20 * lev * nx * ny, 34 << 20),
        name="prepare",
    )(odd, me, blocks, v, cu, cv, k)


def fill_kernel(odd_x, odd_y, inj, got_near, got_far, *refs, lev, nx, nt):
    w, cuf, cvf, kf, own_l, own_r, near, far, known = refs[8:]
    rest = jnp.zeros((SUBL - HALO, LANES), F32)
    flip = odd_x[0] != 0

    def ends(l, j, q, o):
        at = (q * lev + l, slice(o, o + HALO), slice(LANES * j, LANES * (j + 1)))
        x, y = (got_near[at], got_far[at])
        return jnp.where(flip, x, y), jnp.where(flip, y, x)

    def pair(l, j, q, o):
        top, low = ends(l, j, q, o)
        return jnp.concatenate([rest, top], 0), jnp.concatenate([low, rest], 0)

    for end in range(2):
        to = (FRONT + nx) if end else (FRONT - SUBL)
        at = (EDGE + nx) if end else (EDGE - SUBL)

        def store(l, j, x):
            w[l, j, to : to + SUBL, :] = x

        diffuse(
            lambda l: [pair(l, j, 0, 0)[end] for j in range(nt)],
            lambda l, j: pair(l, j, 1, HALO)[end],
            store,
            lev,
            nt,
        )
        for l in range(lev):
            for j in range(nt):
                for buf, q, o in ((cuf, 0, HALO), (cvf, 1, 0), (kf, 1, HALO)):
                    buf[l, j, at : at + SUBL, :] = pair(l, j, q, o)[end]
    packed = []
    for side in range(2):
        take, level = edge_lanes(SUBL, lev, side == 1)
        packed.append([])
        for q, o in ((0, 0), (0, HALO), (1, 0), (1, HALO)):
            slabs = [jnp.concatenate(ends(l, (nt - 1) * side, q, o)[::-1], 0) for l in range(lev)]
            packed[-1].append(pack_edge(slabs, take, level))
    store_edges(packed, (own_l, own_r), near, far, slice(nx, nx + SUBL), odd_y[0] != 0)
    lines = inj.shape[0]
    tail = nx + SUBL
    known[:lines, :] = inj[...].astype(F32)
    known[lines:, :] = got_near[2 * lev, :lines, :LANES]
    for i in range(2):
        near[i, tail:, :] = jnp.zeros((SUBL, LANES), F32)
    near[0, tail : tail + 2 * lines, :] = known[...]


def fill(odd_x, odd_y, inj, got_near, got_far, arrays):
    lev = got_far.shape[0] // 2
    nt = got_far.shape[2] // LANES
    nx = arrays[4].shape[1] - SUBL
    known = jax.ShapeDtypeStruct((2 * inj.shape[0], LANES), F32)
    return pl.pallas_call(
        functools.partial(fill_kernel, lev=lev, nx=nx, nt=nt),
        out_shape=tuple(jax.ShapeDtypeStruct(x.shape, x.dtype) for x in arrays) + (known,),
        in_specs=[SMEM] * 2 + [VMEM] * 11,
        out_specs=(VMEM,) * 9,
        input_output_aliases={5 + i: i for i in range(8)},
        compiler_params=params(3),
        cost_estimate=cost(0, 4 << 20),
        name="fill",
    )(odd_x, odd_y, inj, got_near, got_far, *arrays)


def sweep_kernel(src, cuf, cvf, *refs, lev, nx, nt, last_step):
    dst = refs[-1]
    lane = lane_id((SUBL, LANES))
    first, last = (lane == 0, lane == LANES - 1)

    def advect(l, g):
        mid = [load_group(src, l, j, g) for j in range(nt)]
        nxt = [pltpu.roll(x, LANES - 1, 1) for x in mid]
        prv = [pltpu.roll(x, 1, 1) for x in mid]
        out = []
        for j in range(nt):
            yp = jnp.where(last, nxt[j + 1], nxt[j]) if j + 1 < nt else nxt[j]
            ym = jnp.where(first, prv[j - 1], prv[j]) if j > 0 else prv[j]
            cu, cv = (load_coef(cuf, l, j, g), load_coef(cvf, l, j, g))
            wx = jnp.where(cu > 0, load_group(src, l, j, g, 1), load_group(src, l, j, g, -1))
            wy = jnp.where(cv > 0, yp, ym)
            out.append(mid[j] + jnp.abs(cu) * (wx - mid[j]) + jnp.abs(cv) * (wy - mid[j]))
        return out

    def body(g, _):
        if last_step:
            for l in range(lev):
                for j, x in enumerate(advect(l, g)):
                    dst[j * (nx // SUBL) + g - 1, l] = x
            return 0
        at = pl.ds(pl.multiple_of(g * SUBL + (FRONT - EDGE), SUBL), SUBL)

        def store(l, j, x):
            dst[l, j, at, :] = x

        diffuse(lambda l: advect(l, g), lambda l, j: load_coef(refs[0], l, j, g), store, lev, nt)
        return 0

    groups = nx // SUBL
    lo, hi = (1, groups + 1) if last_step else (0, groups + 2)
    whole = (hi - lo) // UNROLL

    def several(i, _):
        for n in range(UNROLL):
            body(lo + i * UNROLL + n, 0)
        return 0

    lax.fori_loop(0, whole, several, 0)
    for g in range(lo + whole * UNROLL, hi):
        body(g, 0)


def sweep(src, cuf, cvf, kf, last_step):
    lev, nt, rows, _ = src.shape
    nx = rows - 2 * FRONT
    ins = (src, cuf, cvf) if last_step else (src, cuf, cvf, kf)
    shape = (nt * nx // SUBL, lev, SUBL, LANES) if last_step else src.shape
    return pl.pallas_call(
        functools.partial(sweep_kernel, lev=lev, nx=nx, nt=nt, last_step=last_step),
        out_shape=jax.ShapeDtypeStruct(shape, F32),
        in_specs=[VMEM] * len(ins),
        out_specs=VMEM,
        compiler_params=params(3),
        cost_estimate=cost(18 * lev * nt * nx * LANES, 16 << 20),
        name="sweep_last" if last_step else "sweep",
    )(*ins)


def strips_kernel(odd, own_l, own_r, got_near, got_far, out_l, out_r, strip, other, coef, *, lev, nx):
    rows = nx + 2 * HALO
    step = rows
    half = LANES // 2
    lane = lane_id((step, LANES))
    low = lane < half
    top_level = lane % lev == lev - 1
    head, tail = (lane < lev, lane >= LANES - lev)

    def turn(x):
        return pltpu.roll(x, half, 1)

    def gather(n, _):
        at = pl.ds(pl.multiple_of(n * step, SUBL), step)
        put = pl.ds(pl.multiple_of(n * step + SUBL, SUBL), step)
        for a in range(4):
            q = a // 2
            ol, orr = (own_l[a, at, :], own_r[a, at, :])
            x, y = (got_near[q, at, :], got_far[q, at, :])
            gl, gr = (jnp.where(odd[0] != 0, x, y), jnp.where(odd[0] != 0, y, x))
            if a % 2:
                gl = turn(gl)
            else:
                gr = turn(gr)
            parts = (
                jnp.where(low, gl, turn(ol)),
                turn(jnp.where(low, orr, ol)),
                jnp.where(low, turn(orr), gr),
            )
            for i, x in enumerate(parts):
                if a == 0:
                    strip[i, put, :] = x
                elif a == 3:
                    coef[2, i, at, :] = jnp.where(top_level, 0.0, x)
                else:
                    coef[a - 1, i, at, :] = x
        return 0

    lax.fori_loop(0, rows // step, gather, 0)

    def diffuse(n, _):
        at = pl.ds(pl.multiple_of(n * step, SUBL), step)
        put = pl.ds(pl.multiple_of(n * step + SUBL, SUBL), step)
        for i in range(3):
            x = strip[i, put, :]
            f = coef[2, i, at, :] * (pltpu.roll(x, LANES - 1, 1) - x)
            other[i, put, :] = x + f - pltpu.roll(f, 1, 1)
        return 0

    def advect(n, _):
        at = pl.ds(pl.multiple_of(n * step, SUBL), step)
        put = pl.ds(pl.multiple_of(n * step + SUBL, SUBL), step)
        mid = [other[i, put, :] for i in range(3)]
        nxt = [pltpu.roll(x, LANES - lev, 1) for x in mid]
        prv = [pltpu.roll(x, lev, 1) for x in mid]
        yps = (jnp.where(tail, nxt[1], nxt[0]), jnp.where(tail, nxt[2], nxt[1]), nxt[2])
        yms = (prv[0], jnp.where(head, prv[0], prv[1]), jnp.where(head, prv[1], prv[2]))
        for i in range(3):
            cu, cv = (coef[0, i, at, :], coef[1, i, at, :])
            wx = jnp.where(
                cu > 0,
                other[i, pl.ds(n * step + SUBL + 1, step), :],
                other[i, pl.ds(n * step + SUBL - 1, step), :],
            )
            wy = jnp.where(cv > 0, yps[i], yms[i])
            strip[i, put, :] = mid[i] + jnp.abs(cu) * (wx - mid[i]) + jnp.abs(cv) * (wy - mid[i])
        return 0

    for _ in range(ITERS):
        lax.fori_loop(0, rows // step, diffuse, 0)
        for i in range(3):
            other[i, SUBL - 1 : SUBL, :] = other[i, SUBL + rows - 1 : SUBL + rows, :]
            other[i, SUBL + rows : SUBL + rows + 1, :] = other[i, SUBL : SUBL + 1, :]
        lax.fori_loop(0, rows // step, advect, 0)

    out_l[...] = strip[0, SUBL : SUBL + nx, :]
    out_r[...] = strip[2, SUBL : SUBL + nx, :]


def strips(odd, own_l, own_r, got_near, got_far, lev):
    rows = own_l.shape[1]
    nx = rows - 2 * HALO
    out = jax.ShapeDtypeStruct((nx, LANES), F32)
    return pl.pallas_call(
        functools.partial(strips_kernel, lev=lev, nx=nx),
        out_shape=(out, out),
        in_specs=[SMEM] + [VMEM] * 4,
        out_specs=(VMEM, VMEM),
        scratch_shapes=[
            pltpu.VMEM((3, rows + 2 * SUBL, LANES), F32),
            pltpu.VMEM((3, rows + 2 * SUBL, LANES), F32),
            pltpu.VMEM((3, 3, rows, LANES), F32),
        ],
        compiler_params=params(8),
        cost_estimate=cost(10 << 20, 3 << 20),
        name="strips",
    )(odd, own_l, own_r, got_near, got_far)


def finish_kernel(
    me_ref, row, shift, pos, inj, prof, edge_l, edge_r, mid, state, send, field, weight, osem,
    *, lev, nx, nt, cap, procs, order,
):
    def spread(i, _):
        for l in range(lev):
            weight[i, l] = jnp.full((TB, LANES), prof[i, l], F32)
        return 0

    lax.fori_loop(0, lev, spread, 0)
    lane8 = lane_id((SUBL, LANES))
    width = HALO
    outer, inner = (lane8 < width, lane8 >= LANES - width)
    base = (nt - 1) * nx // SUBL

    def patch(n, _):
        for m in range(2):
            l = 2 * n + m
            take_l = (lane8 * lev + (LANES // 2 + l)) & (LANES - 1)
            take_r = ((lane8 - (LANES - width)) * lev + l) & (LANES - 1)
            for g in range(0, nx, SUBL):
                x, y = (edge_l[g : g + SUBL, :], edge_r[g : g + SUBL, :])
                x = jnp.take_along_axis(x, take_l, axis=1)
                y = jnp.take_along_axis(y, take_r, axis=1)
                g //= SUBL
                field[g, l] = jnp.where(outer, x, field[g, l])
                g += base
                field[g, l] = jnp.where(inner, y, field[g, l])
        return 0

    lax.fori_loop(0, lev // 2, patch, 0)
    count = nx // SUBL
    puts = [
        pltpu.make_async_copy(
            field.at[pl.ds(j * count, count), l],
            state.at[l, :, :, pl.ds(j * LANES, LANES)],
            osem.at[j, l],
        )
        for j in range(nt)
        for l in range(lev)
    ]
    for c in puts:
        c.start()
    me = me_ref[0]
    slot_of = lane_id((TB, LANES)) >> TB.bit_length() - 1

    def handler(h):
        out = jnp.zeros((TB, LANES), F32)
        apart = h ^ me
        source = 0
        lines = inj.shape[0] // procs
        for n, bit in enumerate(order):
            source = source | (apart >> bit.bit_length() - 1 & 1) << n
        for s in range(cap):
            at = row[h, s]
            tile = pos[h, s]
            level = inj[source * lines + (tile >> LANES.bit_length() - 1), tile & (LANES - 1)]
            terms = [weight[level, l] * field[at, l] for l in range(lev)]
            while len(terms) > 1:
                terms = [x + y for x, y in zip(terms[::2], terms[1::2])]
            out = jnp.where(slot_of == s, pltpu.roll(terms[0], shift[h, s], 1), out)
        send[h] = out

    def handlers(n, _):
        for m in range(4):
            handler(4 * n + m)
        return 0

    lax.fori_loop(0, procs // 4, handlers, 0)
    for c in puts:
        c.wait()


def finish(me, row, shift, pos, inj, prof, edge_l, edge_r, mid, cap, order):
    lev, nx = (mid.shape[1], edge_l.shape[0])
    nt = mid.shape[0] * SUBL // nx
    procs = row.shape[0]
    state, send, _ = pl.pallas_call(
        functools.partial(finish_kernel, lev=lev, nx=nx, nt=nt, cap=cap, procs=procs, order=order),
        out_shape=(
            jax.ShapeDtypeStruct((lev, nx // SUBL, SUBL, nt * LANES), F32),
            jax.ShapeDtypeStruct((procs, TB, LANES), F32),
            jax.ShapeDtypeStruct(mid.shape, F32),
        ),
        in_specs=[SMEM] * 6 + [VMEM] * 3,
        out_specs=(HBM, VMEM, VMEM),
        input_output_aliases={8: 2},
        scratch_shapes=[pltpu.VMEM((lev, lev, TB, LANES), F32), pltpu.SemaphoreType.DMA((nt, lev))],
        compiler_params=params(4),
        cost_estimate=cost(30 << 20, 20 << 20),
        name="finish",
    )(me, row, shift, pos, inj, prof, edge_l, edge_r, mid)
    return state.reshape(lev, nx, nt * LANES), send


def split3(x):
    hi = x.astype(BF16)
    rest = x - hi.astype(F32)
    mid = rest.astype(BF16)
    return hi, mid, (rest - mid.astype(F32)).astype(BF16)


def gradient_kernel(src, slot, got, burn, out, cols, parts, wide, sem, *, cells, width):
    tiles, fire = burn.shape
    procs = got.shape[0]
    block = min(tiles, 8 * SUBL)
    for a in range(TB):
        parts[a] = jnp.concatenate(split3(got[:, a, :]), 0)
    lane = lane_id((block, LANES))
    low = lane < cells
    which = lane >> TB.bit_length() - 1
    third = lane_id((block, 3 * procs))
    who = jnp.where(third >= procs, third - procs, third)
    who = jnp.where(who >= procs, who - procs, who)

    def rows(n, _):
        at = pl.ds(pl.multiple_of(n * block, block), block)
        pick = jnp.where(who == src[at, :], 1.0, 0.0).astype(BF16)
        keep = which == slot[at, :]
        t = [
            jnp.where(keep, jnp.dot(pick, parts[a], preferred_element_type=F32), 0.0)
            for a in range(TB)
        ]
        w = TB
        while len(t) > 1:
            even = lane & w == 0
            t = [
                jnp.where(even, x, y) + pltpu.roll(jnp.where(even, y, x), w, 1)
                for x, y in zip(t[::2], t[1::2])
            ]
            w *= 2
        col = t[0]
        while w < LANES:
            col = col + pltpu.roll(col, w, 1)
            w *= 2
        hi = col.astype(BF16).astype(F32)
        mid = (col - hi).astype(BF16).astype(F32)
        cols[at, :LANES] = jnp.where(low, hi, mid).astype(BF16)
        cols[at, LANES:] = jnp.where(low, col - hi - mid, 0.0).astype(BF16)
        return 0

    for n in range(tiles // block):
        rows(n, 0)
    c = lax.broadcasted_iota(I32, (cells, width), 0) * SUB
    lane = lane_id((cells, width)) - c
    copies = []
    for n in range(fire // width):
        q = lane + n * width
        spread = jnp.where((q >= 0) & (q < SUB), 1.0, 0.0).astype(BF16)
        at = slice(n * width, (n + 1) * width)
        full = jnp.dot(
            cols[...], jnp.concatenate([spread] * (2 * LANES // cells), 0), preferred_element_type=F32
        )
        wide[:, at] = (burn[:, at].astype(F32) * full).astype(BF16)
        copies.append(pltpu.make_async_copy(wide.at[:, at], out.at[:, at], sem.at[n]))
        copies[-1].start()
    for x in copies:
        x.wait()


def gradient(src, slot, got, burn):
    tiles, fire = burn.shape
    cells = TB * TB
    procs = got.shape[0]
    width = max(w for w in range(LANES, 11 * LANES, LANES) if fire % w == 0)
    return pl.pallas_call(
        functools.partial(gradient_kernel, cells=cells, width=width),
        out_shape=jax.ShapeDtypeStruct((tiles, fire), BF16),
        in_specs=[VMEM] * 4,
        out_specs=HBM,
        scratch_shapes=[
            pltpu.VMEM((tiles, 2 * LANES), BF16),
            pltpu.VMEM((TB, 3 * procs, LANES), BF16),
            pltpu.VMEM((tiles, fire), BF16),
            pltpu.SemaphoreType.DMA((fire // width,)),
        ],
        compiler_params=params(16),
        cost_estimate=cost(2 * tiles * fire * 4 * cells, 7 << 20),
        name="gradient",
    )(src, slot, got, burn)


def exchange(near, far, axis):
    count = lax.axis_size(axis)
    first = lax.ppermute(near, axis, [(i, i ^ 1) for i in range(count)])
    pairs = [(i, i + 1) for i in range(1, count - 1, 2)]
    return first, lax.ppermute(far, axis, pairs + [(j, i) for i, j in pairs])


def bits(count):
    return [1 << n for n in range(count.bit_length() - 1)]


def on_device(
    adjoint_forcing,
    courant_x,
    courant_y,
    vertical_mix,
    tile_block,
    injection_level,
    plume_profile,
    burn_weight,
):
    lev, nx, ny = adjoint_forcing.shape
    gx, gy = (lax.axis_size("gx"), lax.axis_size("gy"))
    procs = gx * gy
    tiles = injection_level.shape[0]
    sources = min(tiles // 4, procs // 2)
    cap = tiles // sources
    me = lax.axis_index(("gx", "gy"))
    me1 = me.astype(I32).reshape(1)
    fields = tuple(
        pltpu.with_memory_space_constraint(x, pltpu.HBM)
        for x in (adjoint_forcing, courant_x, courant_y, vertical_mix)
    )

    steps = [("gx", b) for b in bits(gx)[1:][::-1]] + [("gy", b) for b in bits(gy)[1:][::-1]]
    order = (gy, 1) + tuple(b * gy if axis == "gx" else b for axis, b in steps)
    inj = injection_level.reshape(-1, LANES)

    def widen(known, step):
        axis, bit = step
        pairs = [(i, i ^ bit) for i in range(lax.axis_size(axis))]
        return jnp.concatenate([known, lax.ppermute(known, axis, pairs)], 0)

    odd_x, odd_y = ((lax.axis_index(a).astype(I32) & 1).reshape(1) for a in ("gx", "gy"))
    near, far = pack_x(odd_x, *fields, pltpu.with_memory_space_constraint(inj, pltpu.HBM))
    got_near, got_far = exchange(near, far, "gx")
    ready = prepare(odd_y, me1, tile_block, procs, cap, gy, *fields)
    row, shift, pos, src, slot = ready[8:]
    w, cu, cv, k, own_l, own_r, near, far, known = fill(odd_x, odd_y, inj, got_near, got_far, ready[:8])
    got_near, got_far = exchange(near, far, "gy")
    for n in range(ITERS):
        if n == ITERS // 2:
            w, got_near = lax.optimization_barrier((w, got_near))
            other = got_near[0, nx + SUBL : nx + SUBL + known.shape[0], :]
            known = jnp.concatenate([known, other], 0)
        if n >= ITERS // 2:
            known, w = lax.optimization_barrier((known, w))
            now = 1 if n + 1 < ITERS else len(steps) - 1
            for step in steps[:now]:
                known = widen(known, step)
            steps = steps[now:]
        w = sweep(w, cu, cv, k, n + 1 == ITERS)
    known, w = lax.optimization_barrier((known, w))
    for step in steps:
        known = widen(known, step)
    edge_l, edge_r = strips(odd_y, own_l, own_r, got_near, got_far, lev)
    state, columns = finish(
        me1, row, shift, pos, known.astype(I32), plume_profile, edge_l, edge_r, w, cap, order
    )
    columns = lax.all_to_all(columns, ("gx", "gy"), split_axis=0, concat_axis=0, tiled=True)
    return state, gradient(src, slot, columns, burn_weight)


def solution(mesh):
    return jax.shard_map(
        on_device,
        mesh=mesh,
        in_specs=(
            P(None, "gx", "gy"),
            P(None, "gx", "gy"),
            P(None, "gx", "gy"),
            P(None, "gx", "gy"),
            P(),
            P(("gx", "gy")),
            P(),
            P(("gx", "gy"), None),
        ),
        out_specs=(P(None, "gx", "gy"), P(("gx", "gy"), None)),
        check_vma=False,
    )
```

```python
import functools

import jax
import jax.numpy as jnp
from jax import lax
from jax.experimental import pallas as pl
from jax.experimental.pallas import tpu as pltpu
from jax.sharding import PartitionSpec as P

ITERS = 4
TB = 8
SUB = 100
LANES = 128
SUBL = 8
ROWS = 16
FRONT = 2 * SUBL
EDGE = SUBL
HALO = ITERS
UNROLL = 8

F32 = jnp.float32
BF16 = jnp.bfloat16
I32 = jnp.int32
ANY = pl.BlockSpec(memory_space=pl.ANY)
HBM = pl.BlockSpec(memory_space=pltpu.HBM)
VMEM = pl.BlockSpec(memory_space=pltpu.VMEM)
SMEM = pl.BlockSpec(memory_space=pltpu.SMEM)


def params(mib, **kw):
    return pltpu.CompilerParams(vmem_limit_bytes=mib << 20, **kw)


def cost(flops, nbytes):
    return pl.CostEstimate(flops=flops, bytes_accessed=nbytes, transcendentals=0)


def lane_id(shape):
    return lax.broadcasted_iota(I32, shape, 1)


def pack_x_kernel(odd, vt, vb, cut, cub, cvt, cvb, kt, kb, inj, near, far):
    h, b = (HALO, ROWS)
    lev = vt.shape[0]

    def pack(up, dn):
        def level(l, _):
            up[l] = jnp.concatenate([vt[l, :h], cut[l].astype(F32)[:h]], 0)
            up[lev + l] = jnp.concatenate([cvt[l].astype(F32)[:h], kt[l].astype(F32)[:h]], 0)
            dn[l] = jnp.concatenate([vb[l, SUBL - h :], cub[l].astype(F32)[b - h :]], 0)
            dn[lev + l] = jnp.concatenate([cvb[l].astype(F32)[b - h :], kb[l].astype(F32)[b - h :]], 0)
            return 0

        lax.fori_loop(0, lev, level, 0)

    @pl.when(odd[0] == 0)
    def _():
        pack(far, near)

    @pl.when(odd[0] != 0)
    def _():
        pack(near, far)

    near[2 * lev] = jnp.zeros(near.shape[1:], F32)
    near[2 * lev, : inj.shape[0], :LANES] = inj[...].astype(F32)


def pack_x(odd, v, cu, cv, k, inj):
    lev, nx, ny = v.shape

    def ends(x, rows):
        last = nx // rows - 1
        return (
            pl.BlockSpec((lev, rows, ny), lambda i: (0, 0, 0)),
            pl.BlockSpec((lev, rows, ny), lambda i: (0, last, 0)),
        )

    specs = [s for x, r in ((v, SUBL), (cu, ROWS), (cv, ROWS), (k, ROWS)) for s in ends(x, r)]
    near = (2 * lev + 1, 2 * HALO, ny)
    far = (2 * lev, 2 * HALO, ny)
    return pl.pallas_call(
        pack_x_kernel,
        grid=(1,),
        out_shape=(jax.ShapeDtypeStruct(near, F32), jax.ShapeDtypeStruct(far, F32)),
        in_specs=[SMEM] + specs + [pl.BlockSpec(inj.shape, lambda i: (0, 0))],
        out_specs=(pl.BlockSpec(near, lambda i: (0, 0, 0)), pl.BlockSpec(far, lambda i: (0, 0, 0))),
        compiler_params=params(12),
        cost_estimate=cost(0, 3 << 20),
        name="pack_x",
    )(odd, v, v, cu, cu, cv, cv, k, k, inj)


def edge_lanes(rows, lev, right):
    per = LANES // lev
    lane = lane_id((rows, LANES))
    take = lane // lev + (LANES - per if right else 0)
    return take, lane % lev


def pack_edge(slabs, take, level):
    acc = None
    for l, slab in enumerate(slabs):
        got = jnp.take_along_axis(slab, take, axis=1)
        acc = got if acc is None else jnp.where(level == l, got, acc)
    return acc


def store_edges(packed, owns, near, far, at, odd):
    half = LANES // 2
    low = lane_id(packed[0][0].shape) < half
    rows = owns[0].shape[1]
    for own, arrays in zip(owns, packed):
        for i, x in enumerate(arrays):
            own[i, at, :] = x
    for i in range(2):
        a, b = packed[0][2 * i : 2 * i + 2]
        left = jnp.where(low, a, pltpu.roll(b, half, 1))
        a, b = packed[1][2 * i : 2 * i + 2]
        right = jnp.where(low, pltpu.roll(a, half, 1), b)
        near[i, at, :] = jnp.where(odd, left, right)
        far[i, at, :] = jnp.where(odd, right, left)


def load_group(ref, l, j, g, off=0):
    if off:
        return ref[l, j, pl.ds(g * SUBL + (FRONT - EDGE) + off, SUBL), :]
    return ref[l, j, pl.ds(pl.multiple_of(g * SUBL + (FRONT - EDGE), SUBL), SUBL), :]


def load_coef(ref, l, j, g):
    return ref[l, j, pl.ds(pl.multiple_of(g * SUBL, SUBL), SUBL), :]


def diffuse(get, mix, put, lev, nt):
    cur, below = (get(0), None)
    for l in range(lev):
        nxt = get(l + 1) if l + 1 < lev else None
        flux = []
        for j in range(nt):
            w = cur[j]
            if nxt is not None:
                f = mix(l, j) * (nxt[j] - cur[j])
                flux.append(f)
                w = w + (f - below[j]) if below else w + f
            elif below:
                w = w - below[j]
            put(l, j, w)
        cur, below = (nxt, flux)


def index_kernel(me_ref, blocks, row, shift, pos, src_col, slot_col, *, tiles, per_x, per_y, gy, cap, nx):
    per = tiles // LANES
    procs = blocks.shape[0] // per
    me = me_ref[0]
    per_tile = LANES // TB

    def lines(start, count, stride):
        return jnp.concatenate([blocks[pl.ds(start + i, count, stride), :] for i in range(per)], 1)

    def owner(b):
        br, bc = (b // (per_y * gy), b % (per_y * gy))
        return br // per_x * gy + bc // per_y, br % per_x, bc % per_y

    src, lr, lc = owner(lines(0, procs, per))
    mine = src == me
    t = lane_id((procs, tiles))
    upper = lax.broadcasted_iota(I32, (tiles, tiles), 0) <= lane_id((tiles, tiles))
    rank = jnp.dot(
        mine.astype(F32).astype(BF16), upper.astype(F32).astype(BF16), preferred_element_type=F32
    ).astype(I32)
    code = ((lc // per_tile * (nx // TB) + lr) * per_tile + lc % per_tile) * tiles + t + 1
    lane = lane_id((procs, LANES))
    found = jnp.zeros((procs, LANES), I32)
    for s in range(cap):
        hit = mine & (rank == s + 1)
        one = jnp.sum(jnp.where(hit, code, 0).astype(F32), axis=1, keepdims=True).astype(I32)
        found = jnp.where(lane == s, one, found)
    value = found - 1
    spot = value // tiles
    row[...] = jnp.where(found > 0, spot // per_tile, 0)
    shift[...] = (lane * TB - spot % per_tile * TB) & (LANES - 1)
    pos[...] = jnp.where(found > 0, value % tiles, 0)
    own = owner(lines(me * per, 1, 1))[0]
    i = lax.broadcasted_iota(I32, (tiles, tiles), 0)
    j = lane_id((tiles, tiles))
    own_all = jnp.broadcast_to(own, (tiles, tiles)).astype(F32)
    col = jnp.sum(jnp.where(i == j, own_all, 0.0), axis=1, keepdims=True)
    same = (own_all == col) & (j < i)
    src_col[...] = col.astype(I32)
    slot_col[...] = jnp.sum(jnp.where(same, 1.0, 0.0), axis=1, keepdims=True).astype(I32)


def prepare_kernel(
    odd_ref, me_ref, blocks_hbm, v_hbm, cu_hbm, cv_hbm, k_hbm, w, cuf, cvf, kf, own_l, own_r, near, far,
    row, shift, pos, src_col, slot_col, vs, cus, cvs, ks, blocks, sem, bsem, *, lev, nx, nt, chunks, index,
):
    table = pltpu.make_async_copy(blocks_hbm, blocks, bsem)
    table.start()
    part = nx // chunks
    copies = []
    for c in range(chunks):
        at = pl.ds(c * part, part)
        pairs = ((v_hbm, vs), (k_hbm, ks), (cu_hbm, cus), (cv_hbm, cvs))
        copies.append(
            [
                pltpu.make_async_copy(src.at[:, at, :], dst.at[:, at, :], sem.at[c, i])
                for i, (src, dst) in enumerate(pairs)
            ]
        )
    for group in copies:
        for c in group:
            c.start()
    takes = [edge_lanes(ROWS, lev, side == 1) for side in range(2)]

    def rows(r, _):
        at = pl.ds(pl.multiple_of(r * ROWS, ROWS), ROWS)
        put = pl.ds(pl.multiple_of(r * ROWS + EDGE, SUBL), ROWS)
        here = pl.ds(pl.multiple_of(r * ROWS + FRONT, SUBL), ROWS)
        lanes = [slice(LANES * j, LANES * (j + 1)) for j in range(nt)]
        raws = (vs, cus, cvs, ks)
        bufs = (None, cuf, cvf, kf)
        packed = [[None] * 4, [None] * 4]

        def store(l, j, x):
            w[l, j, here, :] = x
            for i in range(4):
                wide = raws[i][l, at, lanes[j]].astype(F32)
                if i:
                    bufs[i][l, j, put, :] = wide
                for side in range(2):
                    if j == (nt - 1) * side:
                        take, level = takes[side]
                        got = jnp.take_along_axis(wide, take, axis=1)
                        old = packed[side][i]
                        packed[side][i] = got if old is None else jnp.where(level == l, got, old)

        diffuse(
            lambda l: [vs[l, at, lanes[j]] for j in range(nt)],
            lambda l, j: ks[l, at, lanes[j]].astype(F32),
            store,
            lev,
            nt,
        )
        store_edges(packed, (own_l, own_r), near, far, at, odd_ref[0] != 0)
        return 0

    def two(n, _):
        rows(2 * n, 0)
        return rows(2 * n + 1, 0)

    for c in range(chunks):
        for x in copies[c]:
            x.wait()
        lax.fori_loop(c * part // ROWS, (c + 1) * part // ROWS, rows, 0)

    table.wait()
    index_kernel(me_ref, blocks, row, shift, pos, src_col, slot_col, nx=nx, **index)


def prepare(odd, me, tile_block, procs, cap, gy, v, cu, cv, k):
    lev, nx, ny = v.shape
    nt = ny // LANES
    chunks = max(c for c in (1, 2, 3, 4) if nx % (c * ROWS) == 0)
    tiles = tile_block.shape[0] // procs
    blocks = pltpu.with_memory_space_constraint(tile_block.reshape(-1, LANES), pltpu.HBM)
    index = dict(tiles=tiles, per_x=nx // TB, per_y=ny // TB, gy=gy, cap=cap)
    table = jax.ShapeDtypeStruct((procs, LANES), I32)
    column = jax.ShapeDtypeStruct((tiles, 1), I32)
    wide = jax.ShapeDtypeStruct((lev, nt, nx + 2 * EDGE, LANES), F32)
    own = jax.ShapeDtypeStruct((4, nx + SUBL, LANES), F32)
    near = jax.ShapeDtypeStruct((2, nx + 2 * SUBL, LANES), F32)
    far = jax.ShapeDtypeStruct((2, nx + SUBL, LANES), F32)
    return pl.pallas_call(
        functools.partial(prepare_kernel, lev=lev, nx=nx, nt=nt, chunks=chunks, index=index),
        out_shape=(jax.ShapeDtypeStruct((lev, nt, nx + 2 * FRONT, LANES), F32), wide, wide, wide, own, own, near, far)
        + (table,) * 3
        + (column,) * 2,
        in_specs=[SMEM] * 2 + [HBM] * 5,
        out_specs=(VMEM,) * 13,
        scratch_shapes=[pltpu.VMEM((lev, nx, ny), F32)]
        + [pltpu.VMEM((lev, nx, ny), BF16)] * 3
        + [pltpu.VMEM(blocks.shape, I32), pltpu.SemaphoreType.DMA((chunks, 4)), pltpu.SemaphoreType.DMA],
        compiler_params=params(14),
        cost_estimate=cost(20 * lev * nx * ny, 34 << 20),
        name="prepare",
    )(odd, me, blocks, v, cu, cv, k)


def fill_kernel(odd_x, odd_y, inj, got_near, got_far, *refs, lev, nx, nt):
    w, cuf, cvf, kf, own_l, own_r, near, far, known = refs[8:]
    rest = jnp.zeros((SUBL - HALO, LANES), F32)
    flip = odd_x[0] != 0

    def ends(l, j, q, o):
        at = (q * lev + l, slice(o, o + HALO), slice(LANES * j, LANES * (j + 1)))
        x, y = (got_near[at], got_far[at])
        return jnp.where(flip, x, y), jnp.where(flip, y, x)

    def pair(l, j, q, o):
        top, low = ends(l, j, q, o)
        return jnp.concatenate([rest, top], 0), jnp.concatenate([low, rest], 0)

    for end in range(2):
        to = (FRONT + nx) if end else (FRONT - SUBL)
        at = (EDGE + nx) if end else (EDGE - SUBL)

        def store(l, j, x):
            w[l, j, to : to + SUBL, :] = x

        diffuse(
            lambda l: [pair(l, j, 0, 0)[end] for j in range(nt)],
            lambda l, j: pair(l, j, 1, HALO)[end],
            store,
            lev,
            nt,
        )
        for l in range(lev):
            for j in range(nt):
                for buf, q, o in ((cuf, 0, HALO), (cvf, 1, 0), (kf, 1, HALO)):
                    buf[l, j, at : at + SUBL, :] = pair(l, j, q, o)[end]
    packed = []
    for side in range(2):
        take, level = edge_lanes(SUBL, lev, side == 1)
        packed.append([])
        for q, o in ((0, 0), (0, HALO), (1, 0), (1, HALO)):
            slabs = [jnp.concatenate(ends(l, (nt - 1) * side, q, o)[::-1], 0) for l in range(lev)]
            packed[-1].append(pack_edge(slabs, take, level))
    store_edges(packed, (own_l, own_r), near, far, slice(nx, nx + SUBL), odd_y[0] != 0)
    lines = inj.shape[0]
    tail = nx + SUBL
    known[:lines, :] = inj[...].astype(F32)
    known[lines:, :] = got_near[2 * lev, :lines, :LANES]
    for i in range(2):
        near[i, tail:, :] = jnp.zeros((SUBL, LANES), F32)
    near[0, tail : tail + 2 * lines, :] = known[...]


def fill(odd_x, odd_y, inj, got_near, got_far, arrays):
    lev = got_far.shape[0] // 2
    nt = got_far.shape[2] // LANES
    nx = arrays[4].shape[1] - SUBL
    known = jax.ShapeDtypeStruct((2 * inj.shape[0], LANES), F32)
    return pl.pallas_call(
        functools.partial(fill_kernel, lev=lev, nx=nx, nt=nt),
        out_shape=tuple(jax.ShapeDtypeStruct(x.shape, x.dtype) for x in arrays) + (known,),
        in_specs=[SMEM] * 2 + [VMEM] * 11,
        out_specs=(VMEM,) * 9,
        input_output_aliases={5 + i: i for i in range(8)},
        compiler_params=params(3),
        cost_estimate=cost(0, 4 << 20),
        name="fill",
    )(odd_x, odd_y, inj, got_near, got_far, *arrays)


def sweep_kernel(src, cuf, cvf, *refs, lev, nx, nt, last_step):
    dst = refs[-1]
    lane = lane_id((SUBL, LANES))
    first, last = (lane == 0, lane == LANES - 1)

    def advect(l, g):
        mid = [load_group(src, l, j, g) for j in range(nt)]
        nxt = [pltpu.roll(x, LANES - 1, 1) for x in mid]
        prv = [pltpu.roll(x, 1, 1) for x in mid]
        out = []
        for j in range(nt):
            yp = jnp.where(last, nxt[j + 1], nxt[j]) if j + 1 < nt else nxt[j]
            ym = jnp.where(first, prv[j - 1], prv[j]) if j > 0 else prv[j]
            cu, cv = (load_coef(cuf, l, j, g), load_coef(cvf, l, j, g))
            wx = jnp.where(cu > 0, load_group(src, l, j, g, 1), load_group(src, l, j, g, -1))
            wy = jnp.where(cv > 0, yp, ym)
            out.append(mid[j] + jnp.abs(cu) * (wx - mid[j]) + jnp.abs(cv) * (wy - mid[j]))
        return out

    def body(g, _):
        if last_step:
            for l in range(lev):
                for j, x in enumerate(advect(l, g)):
                    dst[j * (nx // SUBL) + g - 1, l] = x
            return 0
        at = pl.ds(pl.multiple_of(g * SUBL + (FRONT - EDGE), SUBL), SUBL)

        def store(l, j, x):
            dst[l, j, at, :] = x

        diffuse(lambda l: advect(l, g), lambda l, j: load_coef(refs[0], l, j, g), store, lev, nt)
        return 0

    groups = nx // SUBL
    lo, hi = (1, groups + 1) if last_step else (0, groups + 2)
    whole = (hi - lo) // UNROLL

    def several(i, _):
        for n in range(UNROLL):
            body(lo + i * UNROLL + n, 0)
        return 0

    lax.fori_loop(0, whole, several, 0)
    for g in range(lo + whole * UNROLL, hi):
        body(g, 0)


def sweep(src, cuf, cvf, kf, last_step):
    lev, nt, rows, _ = src.shape
    nx = rows - 2 * FRONT
    ins = (src, cuf, cvf) if last_step else (src, cuf, cvf, kf)
    shape = (nt * nx // SUBL, lev, SUBL, LANES) if last_step else src.shape
    return pl.pallas_call(
        functools.partial(sweep_kernel, lev=lev, nx=nx, nt=nt, last_step=last_step),
        out_shape=jax.ShapeDtypeStruct(shape, F32),
        in_specs=[VMEM] * len(ins),
        out_specs=VMEM,
        compiler_params=params(3),
        cost_estimate=cost(18 * lev * nt * nx * LANES, 16 << 20),
        name="sweep_last" if last_step else "sweep",
    )(*ins)


def strips_kernel(odd, own_l, own_r, got_near, got_far, out_l, out_r, strip, other, coef, *, lev, nx):
    rows = nx + 2 * HALO
    step = rows
    half = LANES // 2
    lane = lane_id((step, LANES))
    low = lane < half
    top_level = lane % lev == lev - 1
    head, tail = (lane < lev, lane >= LANES - lev)

    def turn(x):
        return pltpu.roll(x, half, 1)

    def gather(n, _):
        at = pl.ds(pl.multiple_of(n * step, SUBL), step)
        put = pl.ds(pl.multiple_of(n * step + SUBL, SUBL), step)
        for a in range(4):
            q = a // 2
            ol, orr = (own_l[a, at, :], own_r[a, at, :])
            x, y = (got_near[q, at, :], got_far[q, at, :])
            gl, gr = (jnp.where(odd[0] != 0, x, y), jnp.where(odd[0] != 0, y, x))
            if a % 2:
                gl = turn(gl)
            else:
                gr = turn(gr)
            parts = (
                jnp.where(low, gl, turn(ol)),
                turn(jnp.where(low, orr, ol)),
                jnp.where(low, turn(orr), gr),
            )
            for i, x in enumerate(parts):
                if a == 0:
                    strip[i, put, :] = x
                elif a == 3:
                    coef[2, i, at, :] = jnp.where(top_level, 0.0, x)
                else:
                    coef[a - 1, i, at, :] = x
        return 0

    lax.fori_loop(0, rows // step, gather, 0)

    def diffuse(n, _):
        at = pl.ds(pl.multiple_of(n * step, SUBL), step)
        put = pl.ds(pl.multiple_of(n * step + SUBL, SUBL), step)
        for i in range(3):
            x = strip[i, put, :]
            f = coef[2, i, at, :] * (pltpu.roll(x, LANES - 1, 1) - x)
            other[i, put, :] = x + f - pltpu.roll(f, 1, 1)
        return 0

    def advect(n, _):
        at = pl.ds(pl.multiple_of(n * step, SUBL), step)
        put = pl.ds(pl.multiple_of(n * step + SUBL, SUBL), step)
        mid = [other[i, put, :] for i in range(3)]
        nxt = [pltpu.roll(x, LANES - lev, 1) for x in mid]
        prv = [pltpu.roll(x, lev, 1) for x in mid]
        yps = (jnp.where(tail, nxt[1], nxt[0]), jnp.where(tail, nxt[2], nxt[1]), nxt[2])
        yms = (prv[0], jnp.where(head, prv[0], prv[1]), jnp.where(head, prv[1], prv[2]))
        for i in range(3):
            cu, cv = (coef[0, i, at, :], coef[1, i, at, :])
            wx = jnp.where(
                cu > 0,
                other[i, pl.ds(n * step + SUBL + 1, step), :],
                other[i, pl.ds(n * step + SUBL - 1, step), :],
            )
            wy = jnp.where(cv > 0, yps[i], yms[i])
            strip[i, put, :] = mid[i] + jnp.abs(cu) * (wx - mid[i]) + jnp.abs(cv) * (wy - mid[i])
        return 0

    for _ in range(ITERS):
        lax.fori_loop(0, rows // step, diffuse, 0)
        for i in range(3):
            other[i, SUBL - 1 : SUBL, :] = other[i, SUBL + rows - 1 : SUBL + rows, :]
            other[i, SUBL + rows : SUBL + rows + 1, :] = other[i, SUBL : SUBL + 1, :]
        lax.fori_loop(0, rows // step, advect, 0)

    out_l[...] = strip[0, SUBL : SUBL + nx, :]
    out_r[...] = strip[2, SUBL : SUBL + nx, :]


def strips(odd, own_l, own_r, got_near, got_far, lev):
    rows = own_l.shape[1]
    nx = rows - 2 * HALO
    out = jax.ShapeDtypeStruct((nx, LANES), F32)
    return pl.pallas_call(
        functools.partial(strips_kernel, lev=lev, nx=nx),
        out_shape=(out, out),
        in_specs=[SMEM] + [VMEM] * 4,
        out_specs=(VMEM, VMEM),
        scratch_shapes=[
            pltpu.VMEM((3, rows + 2 * SUBL, LANES), F32),
            pltpu.VMEM((3, rows + 2 * SUBL, LANES), F32),
            pltpu.VMEM((3, 3, rows, LANES), F32),
        ],
        compiler_params=params(8),
        cost_estimate=cost(10 << 20, 3 << 20),
        name="strips",
    )(odd, own_l, own_r, got_near, got_far)


def finish_kernel(
    me_ref, row, shift, pos, inj, prof, edge_l, edge_r, mid, state, send, field, weight, osem,
    *, lev, nx, nt, cap, procs, order,
):
    def spread(i, _):
        for l in range(lev):
            weight[i, l] = jnp.full((TB, LANES), prof[i, l], F32)
        return 0

    lax.fori_loop(0, lev, spread, 0)
    lane8 = lane_id((SUBL, LANES))
    width = HALO
    outer, inner = (lane8 < width, lane8 >= LANES - width)
    base = (nt - 1) * nx // SUBL

    def patch(n, _):
        for m in range(4):
            l = 4 * n + m
            take_l = (lane8 * lev + (LANES // 2 + l)) & (LANES - 1)
            take_r = ((lane8 - (LANES - width)) * lev + l) & (LANES - 1)
            for g in range(0, nx, SUBL):
                x, y = (edge_l[g : g + SUBL, :], edge_r[g : g + SUBL, :])
                x = jnp.take_along_axis(x, take_l, axis=1)
                y = jnp.take_along_axis(y, take_r, axis=1)
                g //= SUBL
                field[g, l] = jnp.where(outer, x, field[g, l])
                g += base
                field[g, l] = jnp.where(inner, y, field[g, l])
        return 0

    lax.fori_loop(0, lev // 4, patch, 0)
    count = nx // SUBL
    puts = [
        pltpu.make_async_copy(
            field.at[pl.ds(j * count, count), l],
            state.at[l, :, :, pl.ds(j * LANES, LANES)],
            osem.at[j, l],
        )
        for j in range(nt)
        for l in range(lev)
    ]
    for c in puts:
        c.start()
    me = me_ref[0]
    slot_of = lane_id((TB, LANES)) >> TB.bit_length() - 1

    def handler(h):
        out = jnp.zeros((TB, LANES), F32)
        apart = h ^ me
        source = 0
        lines = inj.shape[0] // procs
        for n, bit in enumerate(order):
            source = source | (apart >> bit.bit_length() - 1 & 1) << n
        for s in range(cap):
            at = row[h, s]
            tile = pos[h, s]
            level = inj[source * lines + (tile >> LANES.bit_length() - 1), tile & (LANES - 1)]
            terms = [weight[level, l] * field[at, l] for l in range(lev)]
            while len(terms) > 1:
                terms = [x + y for x, y in zip(terms[::2], terms[1::2])]
            out = jnp.where(slot_of == s, pltpu.roll(terms[0], shift[h, s], 1), out)
        send[h] = out

    def handlers(n, _):
        for m in range(4):
            handler(4 * n + m)
        return 0

    lax.fori_loop(0, procs // 4, handlers, 0)
    for c in puts:
        c.wait()


def finish(me, row, shift, pos, inj, prof, edge_l, edge_r, mid, cap, order):
    lev, nx = (mid.shape[1], edge_l.shape[0])
    nt = mid.shape[0] * SUBL // nx
    procs = row.shape[0]
    state, send, _ = pl.pallas_call(
        functools.partial(finish_kernel, lev=lev, nx=nx, nt=nt, cap=cap, procs=procs, order=order),
        out_shape=(
            jax.ShapeDtypeStruct((lev, nx // SUBL, SUBL, nt * LANES), F32),
            jax.ShapeDtypeStruct((procs, TB, LANES), F32),
            jax.ShapeDtypeStruct(mid.shape, F32),
        ),
        in_specs=[SMEM] * 6 + [VMEM] * 3,
        out_specs=(HBM, VMEM, VMEM),
        input_output_aliases={8: 2},
        scratch_shapes=[pltpu.VMEM((lev, lev, TB, LANES), F32), pltpu.SemaphoreType.DMA((nt, lev))],
        compiler_params=params(4),
        cost_estimate=cost(30 << 20, 20 << 20),
        name="finish",
    )(me, row, shift, pos, inj, prof, edge_l, edge_r, mid)
    return state.reshape(lev, nx, nt * LANES), send


def split3(x):
    hi = x.astype(BF16)
    rest = x - hi.astype(F32)
    mid = rest.astype(BF16)
    return hi, mid, (rest - mid.astype(F32)).astype(BF16)


def gradient_kernel(src, slot, got, burn, out, cols, parts, wide, sem, *, cells, width):
    tiles, fire = burn.shape
    procs = got.shape[0]
    block = min(tiles, 8 * SUBL)
    for a in range(TB):
        parts[a] = jnp.concatenate(split3(got[:, a, :]), 0)
    lane = lane_id((block, LANES))
    low = lane < cells
    which = lane >> TB.bit_length() - 1
    third = lane_id((block, 3 * procs))
    who = jnp.where(third >= procs, third - procs, third)
    who = jnp.where(who >= procs, who - procs, who)

    def rows(n, _):
        at = pl.ds(pl.multiple_of(n * block, block), block)
        pick = jnp.where(who == src[at, :], 1.0, 0.0).astype(BF16)
        keep = which == slot[at, :]
        t = [
            jnp.where(keep, jnp.dot(pick, parts[a], preferred_element_type=F32), 0.0)
            for a in range(TB)
        ]
        w = TB
        while len(t) > 1:
            even = lane & w == 0
            t = [
                jnp.where(even, x, y) + pltpu.roll(jnp.where(even, y, x), w, 1)
                for x, y in zip(t[::2], t[1::2])
            ]
            w *= 2
        col = t[0]
        while w < LANES:
            col = col + pltpu.roll(col, w, 1)
            w *= 2
        hi = col.astype(BF16).astype(F32)
        mid = (col - hi).astype(BF16).astype(F32)
        cols[at, :LANES] = jnp.where(low, hi, mid).astype(BF16)
        cols[at, LANES:] = jnp.where(low, col - hi - mid, 0.0).astype(BF16)
        return 0

    for n in range(tiles // block):
        rows(n, 0)
    c = lax.broadcasted_iota(I32, (cells, width), 0) * SUB
    lane = lane_id((cells, width)) - c
    copies = []
    for n in range(fire // width):
        q = lane + n * width
        spread = jnp.where((q >= 0) & (q < SUB), 1.0, 0.0).astype(BF16)
        at = slice(n * width, (n + 1) * width)
        full = jnp.dot(
            cols[...], jnp.concatenate([spread] * (2 * LANES // cells), 0), preferred_element_type=F32
        )
        wide[:, at] = (burn[:, at].astype(F32) * full).astype(BF16)
        copies.append(pltpu.make_async_copy(wide.at[:, at], out.at[:, at], sem.at[n]))
        copies[-1].start()
    for x in copies:
        x.wait()


def gradient(src, slot, got, burn):
    tiles, fire = burn.shape
    cells = TB * TB
    procs = got.shape[0]
    width = max(w for w in range(LANES, 11 * LANES, LANES) if fire % w == 0)
    return pl.pallas_call(
        functools.partial(gradient_kernel, cells=cells, width=width),
        out_shape=jax.ShapeDtypeStruct((tiles, fire), BF16),
        in_specs=[VMEM] * 4,
        out_specs=HBM,
        scratch_shapes=[
            pltpu.VMEM((tiles, 2 * LANES), BF16),
            pltpu.VMEM((TB, 3 * procs, LANES), BF16),
            pltpu.VMEM((tiles, fire), BF16),
            pltpu.SemaphoreType.DMA((fire // width,)),
        ],
        compiler_params=params(16),
        cost_estimate=cost(2 * tiles * fire * 4 * cells, 7 << 20),
        name="gradient",
    )(src, slot, got, burn)


def exchange(near, far, axis):
    count = lax.axis_size(axis)
    first = lax.ppermute(near, axis, [(i, i ^ 1) for i in range(count)])
    pairs = [(i, i + 1) for i in range(1, count - 1, 2)]
    return first, lax.ppermute(far, axis, pairs + [(j, i) for i, j in pairs])


def bits(count):
    return [1 << n for n in range(count.bit_length() - 1)]


def on_device(
    adjoint_forcing,
    courant_x,
    courant_y,
    vertical_mix,
    tile_block,
    injection_level,
    plume_profile,
    burn_weight,
):
    lev, nx, ny = adjoint_forcing.shape
    gx, gy = (lax.axis_size("gx"), lax.axis_size("gy"))
    procs = gx * gy
    tiles = injection_level.shape[0]
    sources = min(tiles // 4, procs // 2)
    cap = tiles // sources
    me = lax.axis_index(("gx", "gy"))
    me1 = me.astype(I32).reshape(1)
    fields = tuple(
        pltpu.with_memory_space_constraint(x, pltpu.HBM)
        for x in (adjoint_forcing, courant_x, courant_y, vertical_mix)
    )

    steps = [("gx", b) for b in bits(gx)[1:][::-1]] + [("gy", b) for b in bits(gy)[1:][::-1]]
    order = (gy, 1) + tuple(b * gy if axis == "gx" else b for axis, b in steps)
    inj = injection_level.reshape(-1, LANES)

    def widen(known, step):
        axis, bit = step
        pairs = [(i, i ^ bit) for i in range(lax.axis_size(axis))]
        return jnp.concatenate([known, lax.ppermute(known, axis, pairs)], 0)

    odd_x, odd_y = ((lax.axis_index(a).astype(I32) & 1).reshape(1) for a in ("gx", "gy"))
    near, far = pack_x(odd_x, *fields, pltpu.with_memory_space_constraint(inj, pltpu.HBM))
    got_near, got_far = exchange(near, far, "gx")
    ready = prepare(odd_y, me1, tile_block, procs, cap, gy, *fields)
    row, shift, pos, src, slot = ready[8:]
    w, cu, cv, k, own_l, own_r, near, far, known = fill(odd_x, odd_y, inj, got_near, got_far, ready[:8])
    got_near, got_far = exchange(near, far, "gy")
    for n in range(ITERS):
        if n == ITERS // 2:
            w, got_near = lax.optimization_barrier((w, got_near))
            other = got_near[0, nx + SUBL : nx + SUBL + known.shape[0], :]
            known = jnp.concatenate([known, other], 0)
        if n >= ITERS // 2:
            known, w = lax.optimization_barrier((known, w))
            now = 1 if n + 1 < ITERS else len(steps) - 1
            for step in steps[:now]:
                known = widen(known, step)
            steps = steps[now:]
        w = sweep(w, cu, cv, k, n + 1 == ITERS)
    known, w = lax.optimization_barrier((known, w))
    for step in steps:
        known = widen(known, step)
    edge_l, edge_r = strips(odd_y, own_l, own_r, got_near, got_far, lev)
    state, columns = finish(
        me1, row, shift, pos, known.astype(I32), plume_profile, edge_l, edge_r, w, cap, order
    )
    columns = lax.all_to_all(columns, ("gx", "gy"), split_axis=0, concat_axis=0, tiled=True)
    return state, gradient(src, slot, columns, burn_weight)


def solution(mesh):
    return jax.shard_map(
        on_device,
        mesh=mesh,
        in_specs=(
            P(None, "gx", "gy"),
            P(None, "gx", "gy"),
            P(None, "gx", "gy"),
            P(None, "gx", "gy"),
            P(),
            P(("gx", "gy")),
            P(),
            P(("gx", "gy"), None),
        ),
        out_specs=(P(None, "gx", "gy"), P(("gx", "gy"), None)),
        check_vma=False,
    )
```
